256 devices in a mesh: fsdp: 8 (over z_hi, y), tensor: 32 (over x, z_lo, core).
Axes of the slice: x: 4, y: 4, z: 8 (z_hi: 2, z_lo: 4; z = z_hi * 4 + z_lo), core: 2. Of those that a mesh axis runs over, the one named last changes fastest.
Arguments:
- momentum: bfloat16 [8192, 28672], P('fsdp', 'tensor'), may hold values from -6 to 6
- gradient: bfloat16 [8192, 28672], P('fsdp', 'tensor'), may hold values from -4 to 4
- factor: float32 [28672, 512], P('tensor', 'fsdp'), may hold values from -0.03125 to 0.03125
Outputs:
- new_momentum: bfloat16 [8192, 28672], P('fsdp', 'tensor')
- new_factor: float32 [28672, 512], P('tensor', 'fsdp')
- update: bfloat16 [8192, 28672], P('fsdp', 'tensor')
The draws below stay inside these ranges and needn't reach their ends.
All inputs are finite; a program needn't handle non-finite values.
Results may differ from the reference program's by a relative error of at most 0.017.
Values may be sent and summed in bfloat16 or wider, within the bound.
No kernel may reach another device: no remote copies, remote signals or barrier semaphores. Data moves between devices by JAX's collectives and lax.ppermute only.
A program may use at most 64 MiB of HBM per device.

```python
import jax
import jax.numpy as jnp
from jax import lax

D = 8192
FF = 28672
R = 512


def steps_of(own_key, shape, shards, smallest, top_value):
    level = 1.0
    for dim, parts in shards:
        heights = jax.random.uniform(jax.random.fold_in(jax.random.fold_in(own_key, 6), dim), (parts,), jnp.float32, smallest / len(shards), top_value / len(shards))
        level = level * jnp.repeat(jnp.exp(heights), shape[dim] // parts).reshape((-1,) + (1,) * (len(shape) - 1 - dim))
    return level


def noise(own_key, extent, scale, most, pieces=(), held_as=jnp.bfloat16):
    result = jax.random.normal(own_key, extent, jnp.float32) * scale
    if len(pieces) > 0:
        result = steps_of(own_key, extent, pieces, -0.22, 0.18) * result
    return jnp.clip(result, min=-most, max=most).astype(held_as)


def setup_inputs(seed: int = 0) -> dict:
    splits = jax.random.split(jax.random.key(seed), 4)
    momentum = noise(splits[0], (D, FF), 1.0, 6.0, ((0, 8), (1, 32)))
    gradient = noise(splits[1], (D, FF), 0.5, 4.0, ((0, 8), (1, 32)))
    factor = noise(splits[2], (FF, R), FF ** -0.5, 0.03125, ((0, 32), (1, 8)), jnp.float32)
    return dict(momentum=momentum, gradient=gradient, factor=factor)


decay_rate = 0.95
epsilon = 1e-06

def reference(momentum, gradient, factor):
    blended = (momentum.astype(jnp.float32) + gradient.astype(jnp.float32)).astype(jnp.bfloat16)
    lowered = factor.astype(jnp.bfloat16)
    left_factor = jnp.dot(blended.astype(jnp.float32), lowered.astype(jnp.float32), preferred_element_type=jnp.float32)
    gram_matrix = lax.dot_general(left_factor, left_factor, (((0,), (0,)), ((), ())), precision=lax.Precision.HIGHEST)
    lower_factor = jnp.linalg.cholesky(gram_matrix)
    solved = jax.scipy.linalg.solve_triangular(lower_factor, left_factor.T, lower=True)
    orthonormal = solved.T.astype(jnp.bfloat16)
    right_factor = lax.dot_general(blended.astype(jnp.float32), orthonormal.astype(jnp.float32), (((0,), (0,)), ((), ())), preferred_element_type=jnp.float32)
    inverse = lax.rsqrt(lax.optimization_barrier(jnp.sum(right_factor * right_factor, axis=0)) + epsilon)
    new_factor = right_factor * inverse[None, :]
    product = lax.dot_general(orthonormal.astype(jnp.float32), right_factor.astype(jnp.bfloat16).astype(jnp.float32), (((1,), (1,)), ((), ())), preferred_element_type=jnp.float32)
    new_momentum = (blended.astype(jnp.float32) - (1.0 - decay_rate) * product).astype(jnp.bfloat16)
    stepped = lax.dot_general(orthonormal.astype(jnp.float32), new_factor.astype(jnp.bfloat16).astype(jnp.float32), (((1,), (1,)), ((), ())), preferred_element_type=jnp.float32)
    update = (stepped * jnp.sqrt(jnp.float32(D * FF / R))).astype(jnp.bfloat16)
    return (new_momentum, new_factor, update)
```

```python
import jax
import jax.numpy as jnp
from jax import lax
from jax.experimental import pallas as pl
from jax.experimental.pallas import tpu as pltpu
from jax.sharding import Mesh
from jax.sharding import PartitionSpec as P

D = 8192
FF = 28672
R = 512
FAR = 16
BLOCK = 128
BLOCKS = R // BLOCK
PAIRS = [(i, j) for i in range(BLOCKS) for j in range(i + 1)]
SUB = 8
TENSOR = ("far", "core")

decay_rate = 0.95
epsilon = 1e-06
f32 = jnp.float32
bf16 = jnp.bfloat16


def product(left, right, left_dim, right_dim, precision=None):
    return lax.dot_general(
        left, right, (((left_dim,), (right_dim,)), ((), ())), precision=precision, preferred_element_type=f32
    )


def exact(left, right, left_dim, right_dim):
    return product(left, right, left_dim, right_dim, lax.Precision.HIGHEST)


def added(terms):
    while len(terms) > 1:
        terms = [
            terms[i] + terms[i + 1] if i + 1 < len(terms) else terms[i] for i in range(0, len(terms), 2)
        ]
    return terms[0]


def spread(value):
    return jnp.broadcast_to(value, (SUB, BLOCK))


def small_inverse(entries):
    rest = [row[:] for row in entries]
    inverse = [None] * SUB
    upper = [[None] * SUB for _ in range(SUB)]
    for j in range(SUB):
        inverse[j] = lax.rsqrt(rest[j][j])
        for k in range(j + 1, SUB):
            upper[j][k] = rest[j][k] * inverse[j]
        for i in range(j + 1, SUB):
            for k in range(i, SUB):
                rest[i][k] = rest[i][k] - upper[j][i] * upper[j][k]
    result = [[None] * SUB for _ in range(SUB)]
    for j in range(SUB):
        result[j][j] = inverse[j]
        for i in range(j + 1, SUB):
            total = upper[j][i] * result[j][j]
            for k in range(j + 1, i):
                total = total + upper[k][i] * result[k][j]
            result[i][j] = -(inverse[i] * total)
    return result


def factor_block(held):
    sub = lax.broadcasted_iota(jnp.int32, (SUB, BLOCK), 0)
    rows = held[0:SUB, :]
    for panel in range(BLOCK // SUB):
        lo = panel * SUB
        left, right = rows[:, :BLOCK], rows[:, BLOCK:]
        entries = [[None] * SUB for _ in range(SUB)]
        for i in range(SUB):
            for k in range(i, SUB):
                entries[i][k] = spread(left[i : i + 1, lo + k : lo + k + 1])
        inverse = small_inverse(entries)
        columns = []
        for k in range(SUB):
            column = jnp.zeros((SUB, BLOCK), f32)
            for i in range(k, SUB):
                column = jnp.where(sub == i, inverse[i][k], column)
            columns.append(column)
        left = added([columns[k] * spread(left[k : k + 1, :]) for k in range(SUB)])
        right = added([columns[k] * spread(right[k : k + 1, :]) for k in range(SUB)])
        held[lo : lo + SUB, :BLOCK] = left
        held[lo : lo + SUB, BLOCK:] = right
        both = jnp.concatenate([left, right], axis=1)
        if lo + SUB < BLOCK:
            following = held[lo + SUB : lo + 2 * SUB, :]
            across = [spread(following[:, lo + k : lo + k + 1]) for k in range(SUB)]
            weights = [added([across[k] * inverse[i][k] for k in range(i + 1)]) for i in range(SUB)]
            next_left = following[:, :BLOCK] - added([weights[i] * spread(left[i : i + 1, :]) for i in range(SUB)])
            next_right = following[:, BLOCK:] - added([weights[i] * spread(right[i : i + 1, :]) for i in range(SUB)])
            rows = jnp.concatenate([next_left, next_right], axis=1)
        if lo + 2 * SUB < BLOCK:
            change = exact(left, both, 0, 0)
            held[lo + 2 * SUB :, :] = held[lo + 2 * SUB :, :] - change[lo + 2 * SUB :, :]


def inverse_kernel(gram_ref, high_ref, low_ref, gram, inverse, held):
    place = {pair: n for n, pair in enumerate(PAIRS)}
    gram[...] = gram_ref[...]
    inverse[...] = jnp.zeros((R, R), f32)
    row = lax.broadcasted_iota(jnp.int32, (BLOCK, BLOCK), 0)
    column = lax.broadcasted_iota(jnp.int32, (BLOCK, BLOCK), 1)
    identity = jnp.where(row == column, 1.0, 0.0).astype(f32)
    for b in range(BLOCKS):
        lo, hi = b * BLOCK, (b + 1) * BLOCK
        held[:, :BLOCK] = gram[place[b, b]]
        held[:, BLOCK:] = identity
        factor_block(held)
        own = held[:, BLOCK:]
        if b:
            inverse[lo:hi, :lo] = exact(own, inverse[lo:hi, :lo], 1, 0)
        inverse[lo:hi, lo:hi] = own
        lower = {i: exact(gram[place[i, b]], own, 1, 1) for i in range(b + 1, BLOCKS)}
        for i in range(b + 1, BLOCKS):
            for j in range(b + 1, i + 1):
                gram[place[i, j]] = gram[place[i, j]] - exact(lower[i], lower[j], 1, 1)
            into = slice(i * BLOCK, (i + 1) * BLOCK)
            inverse[into, :hi] = inverse[into, :hi] - exact(lower[i], inverse[lo:hi, :hi], 1, 0)
    high = inverse[...].astype(bf16)
    high_ref[...] = high
    low_ref[...] = (inverse[...] - high.astype(f32)).astype(bf16)


def inverse_factor(packed):
    whole = pl.BlockSpec(memory_space=pltpu.VMEM)
    return pl.pallas_call(
        inverse_kernel,
        out_shape=[jax.ShapeDtypeStruct((R, R), bf16)] * 2,
        in_specs=[whole],
        out_specs=[whole] * 2,
        scratch_shapes=[
            pltpu.VMEM((len(PAIRS), BLOCK, BLOCK), f32),
            pltpu.VMEM((R, R), f32),
            pltpu.VMEM((BLOCK, 2 * BLOCK), f32),
        ],
        compiler_params=pltpu.CompilerParams(vmem_limit_bytes=32 << 20),
        cost_estimate=pl.CostEstimate(flops=2 * R**3, bytes_accessed=2 << 20, transcendentals=R),
    )(packed)


def from_everyone(value, axis):
    length = lax.axis_size(axis)
    return lax.all_to_all(jnp.broadcast_to(value[None], (length, *value.shape)), axis, 0, 0, tiled=True)


def swapped(value):
    return lax.ppermute(value, "core", [(0, 1), (1, 0)])


def in_order(own, other, core):
    first = jnp.where(core == 0, own, other)
    second = jnp.where(core == 0, other, own)
    return jnp.concatenate([first, second])


def on_device(momentum, gradient, factor):
    core, far, row_group = lax.axis_index("core"), lax.axis_index("far"), lax.axis_index("fsdp")
    columns = factor.shape[1]
    lowered = factor.T.astype(bf16)
    all_lowered = from_everyone(lowered, "fsdp").reshape(R, -1)
    blended = (momentum.astype(f32) + gradient.astype(f32)).astype(bf16)
    half = blended.shape[0] // 2
    own_rows = lax.dynamic_slice_in_dim(blended, core * half, half, 0)
    other_rows = lax.dynamic_slice_in_dim(blended, (1 - core) * half, half, 0)

    sent = product(other_rows, all_lowered, 1, 1).astype(bf16)
    arrived = swapped(sent)
    partial_left = (product(own_rows, all_lowered, 1, 1) + arrived.astype(f32)).astype(bf16)
    pieces = lax.all_to_all(partial_left.reshape(FAR, -1, R), "far", 0, 0, tiled=True)
    left_rows = jnp.sum(pieces.astype(f32), axis=0).astype(bf16)
    own_left = from_everyone(left_rows, "far").reshape(half, R)
    other_left = swapped(own_left)
    left_factor = in_order(own_left, other_left, core)

    local_gram = product(left_factor, left_factor, 0, 0)
    packed = jnp.concatenate(
        [local_gram[i * BLOCK : (i + 1) * BLOCK, j * BLOCK : (j + 1) * BLOCK] for i, j in PAIRS]
    )
    share = packed.shape[0] // (2 * FAR)
    piece = lax.dynamic_slice_in_dim(packed, (core * FAR + far) * share, share, 0)
    summed = jnp.sum(from_everyone(piece, "fsdp"), axis=0)
    own_gram = from_everyone(summed, "far").reshape(-1, BLOCK)
    gram_matrix = in_order(own_gram, swapped(own_gram), core).reshape(len(PAIRS), BLOCK, BLOCK)
    high, low = inverse_factor(gram_matrix)

    partial_right = product(left_factor, blended, 0, 0).astype(bf16)
    arrived = lax.all_to_all(partial_right.reshape(8, columns, -1), "fsdp", 0, 0, tiled=True)
    right_rows = jnp.sum(arrived.astype(f32), axis=0).astype(bf16)
    raw_right = from_everyone(right_rows, "fsdp").reshape(R, -1)

    right_factor = product(high, raw_right, 1, 0) + product(low, raw_right, 1, 0)
    orthonormal = (product(left_factor, high, 1, 1) + product(left_factor, low, 1, 1)).astype(bf16)
    square_sums = jnp.sum(from_everyone(jnp.sum(right_factor * right_factor, axis=1)[None], TENSOR), axis=(0, 1))
    inverse = lax.rsqrt(square_sums + epsilon)[:, None]
    full_factor = right_factor * inverse
    own_factor = lax.dynamic_slice_in_dim(full_factor, row_group * columns, columns, 0).T
    taken = product(orthonormal, right_factor.astype(bf16), 1, 0)
    stepped = product(orthonormal, full_factor.astype(bf16), 1, 0)
    new_momentum = (blended.astype(f32) - (1.0 - decay_rate) * taken).astype(bf16)
    update = (stepped * jnp.sqrt(f32(D * FF / R))).astype(bf16)
    return (new_momentum, own_factor, update)


def solution(mesh):
    torus = Mesh(mesh.devices.reshape(mesh.shape["fsdp"], FAR, 2), ("fsdp", "far", "core"))
    return jax.shard_map(
        on_device,
        mesh=torus,
        in_specs=(P("fsdp", TENSOR), P("fsdp", TENSOR), P(TENSOR, "fsdp")),
        out_specs=(P("fsdp", TENSOR), P(TENSOR, "fsdp"), P("fsdp", TENSOR)),
        check_vma=False,
    )
```

```python
import jax
import jax.numpy as jnp
from jax import lax
from jax.experimental import pallas as pl
from jax.experimental.pallas import tpu as pltpu
from jax.sharding import Mesh
from jax.sharding import PartitionSpec as P

D = 8192
FF = 28672
R = 512
FAR = 16
BLOCK = 128
BLOCKS = R // BLOCK
PAIRS = [(i, j) for i in range(BLOCKS) for j in range(i + 1)]
SHARE = len(PAIRS) * BLOCK // (2 * FAR)
SUB = 8
TENSOR = ("x", "z_lo", "core")

decay_rate = 0.95
epsilon = 1e-06
f32 = jnp.float32
bf16 = jnp.bfloat16


def product(left, right, left_dim, right_dim):
    return lax.dot_general(left, right, (((left_dim,), (right_dim,)), ((), ())), preferred_element_type=f32)


def added(terms):
    while len(terms) > 1:
        terms = [
            terms[i] + terms[i + 1] if i + 1 < len(terms) else terms[i] for i in range(0, len(terms), 2)
        ]
    return terms[0]


def spread(value):
    return jnp.broadcast_to(value, (SUB, BLOCK))


def small_inverse(entries):
    rest = [row[:] for row in entries]
    inverse = [None] * SUB
    upper = [[None] * SUB for _ in range(SUB)]
    for j in range(SUB):
        inverse[j] = lax.rsqrt(rest[j][j])
        for k in range(j + 1, SUB):
            upper[j][k] = rest[j][k] * inverse[j]
        for i in range(j + 1, SUB):
            for k in range(i, SUB):
                rest[i][k] = rest[i][k] - upper[j][i] * upper[j][k]
    result = [[None] * SUB for _ in range(SUB)]
    for j in range(SUB):
        result[j][j] = inverse[j]
        for i in range(j + 1, SUB):
            total = upper[j][i] * result[j][j]
            for k in range(j + 1, i):
                total = total + upper[k][i] * result[k][j]
            result[i][j] = -(inverse[i] * total)
    return result


def in_three(value):
    first = value.astype(bf16)
    rest = value - first.astype(f32)
    second = rest.astype(bf16)
    return first, second, (rest - second.astype(f32)).astype(bf16)


def exact(left, right, left_dim, right_dim):
    a, b, c = in_three(left)
    d, e, f = in_three(right)
    lefts = jnp.concatenate([a, a, b, b, a, c], axis=left_dim)
    rights = jnp.concatenate([d, e, d, e, f, d], axis=right_dim)
    return product(lefts, rights, left_dim, right_dim)


def factor_block(held):
    sub = lax.broadcasted_iota(jnp.int32, (SUB, BLOCK), 0)
    lane = lax.broadcasted_iota(jnp.int32, (SUB, BLOCK), 1)
    lane_row = lax.broadcasted_iota(jnp.int32, (1, BLOCK), 1)
    rows = held[0:SUB, :]
    for lo in range(0, BLOCK, SUB):
        hi = lo + SUB
        lanes = [spread(rows[:, lo + k : lo + k + 1]) for k in range(SUB)]
        entries = [[spread(lanes[k][i : i + 1, :]) if k >= i else None for k in range(SUB)] for i in range(SUB)]
        inverse = small_inverse(entries)
        columns = []
        for k in range(SUB):
            column = jnp.zeros((SUB, BLOCK), f32)
            for i in range(k, SUB):
                column = jnp.where(sub == i, inverse[i][k], column)
            columns.append(column)
        inside = (lane >= lo) & (lane < hi)
        rows = jnp.where(inside, jnp.where(lane - lo == sub, 1.0, 0.0), rows)
        done = added([columns[k] * spread(rows[k : k + 1, :]) for k in range(SUB)])
        held[lo:hi, :] = done
        if hi < BLOCK:
            following = held[hi : hi + SUB, :]
            across = [spread(following[:, lo + k : lo + k + 1]) for k in range(SUB)]
            weights = [added([across[k] * inverse[i][k] for k in range(i + 1)]) for i in range(SUB)]
            rows = jnp.where(inside, 0.0, following) - added(
                [weights[i] * spread(done[i : i + 1, :]) for i in range(SUB)]
            )
        if hi + SUB < BLOCK:
            change = exact(done, done, 0, 0)
            kept = jnp.where((lane_row >= lo) & (lane_row < hi), 0.0, held[hi + SUB :, :])
            held[hi + SUB :, :] = kept - change[hi + SUB :, :]


def inverse_kernel(place_ref, own_ref, other_ref, high_ref, low_ref, gram, inverse, held):
    first = {pair: n * BLOCK for n, pair in enumerate(PAIRS)}
    for n in range(2 * FAR):
        source = own_ref if n < FAR else other_ref
        into = pl.multiple_of(place_ref[n] * SHARE, SUB)
        gram[pl.ds(into, SHARE), :] = source[(n % FAR) * SHARE : (n % FAR + 1) * SHARE, :]

    def block(i, j):
        return gram[first[i, j] : first[i, j] + BLOCK, :]

    inverse[...] = jnp.zeros((R, R), f32)
    row = lax.broadcasted_iota(jnp.int32, (BLOCK, BLOCK), 0)
    column = lax.broadcasted_iota(jnp.int32, (BLOCK, BLOCK), 1)
    for b in range(BLOCKS):
        lo, hi = b * BLOCK, (b + 1) * BLOCK
        held[...] = block(b, b)
        factor_block(held)
        own = jnp.where(column <= row, held[...], 0.0)
        if b:
            inverse[lo:hi, :lo] = exact(own, inverse[lo:hi, :lo], 1, 0)
        inverse[lo:hi, lo:hi] = own
        lower = {i: exact(block(i, b), own, 1, 1) for i in range(b + 1, BLOCKS)}
        for i in range(b + 1, BLOCKS):
            for j in range(b + 1, i + 1):
                gram[first[i, j] : first[i, j] + BLOCK, :] = block(i, j) - exact(lower[i], lower[j], 1, 1)
            into = slice(i * BLOCK, (i + 1) * BLOCK)
            inverse[into, :hi] = inverse[into, :hi] - exact(lower[i], inverse[lo:hi, :hi], 1, 0)
    high = inverse[...].astype(bf16)
    high_ref[...] = high
    low_ref[...] = (inverse[...] - high.astype(f32)).astype(bf16)


def inverse_factor(place, own, other):
    whole = pl.BlockSpec(memory_space=pltpu.VMEM)
    return pl.pallas_call(
        inverse_kernel,
        out_shape=[jax.ShapeDtypeStruct((R, R), bf16)] * 2,
        in_specs=[pl.BlockSpec(memory_space=pltpu.SMEM), whole, whole],
        out_specs=[whole] * 2,
        scratch_shapes=[
            pltpu.VMEM((len(PAIRS) * BLOCK, BLOCK), f32),
            pltpu.VMEM((R, R), f32),
            pltpu.VMEM((BLOCK, BLOCK), f32),
        ],
        compiler_params=pltpu.CompilerParams(vmem_limit_bytes=32 << 20),
        cost_estimate=pl.CostEstimate(flops=2 * R**3, bytes_accessed=2 << 20, transcendentals=R),
    )(place, own, other)


def from_everyone(value, axis):
    length = lax.axis_size(axis)
    return lax.all_to_all(jnp.broadcast_to(value[None], (length, *value.shape)), axis, 0, 0, tiled=True)


def from_ahead(value, axis, steps):
    length = lax.axis_size(axis)
    return lax.ppermute(value, axis, [(i, (i - steps) % length) for i in range(length)])


def ahead(value, axis):
    return [value] + [from_ahead(value, axis, steps) for steps in range(1, lax.axis_size(axis))]


def from_diagonal(value, steps):
    pairs = [(i, (1 - i // 4) * 4 + (i - steps) % 4) for i in range(8)]
    return lax.ppermute(value, ("z_hi", "y"), pairs)


def turned(pieces, index):
    count, length = len(pieces), pieces[0].shape[0]
    doubled = jnp.concatenate(pieces + pieces[:-1])
    start = lax.rem(count - index, count) * length
    return lax.dynamic_slice_in_dim(doubled, start, count * length, 0)


def in_order(own, other, core):
    first = jnp.where(core == 0, own, other)
    second = jnp.where(core == 0, other, own)
    return jnp.concatenate([first, second])


def on_device(momentum, gradient, factor):
    z_hi, y, x, z_lo, core = (lax.axis_index(name) for name in ("z_hi", "y", "x", "z_lo", "core"))
    columns = factor.shape[1]
    lowered = factor.T.astype(bf16)
    across = from_ahead(lowered, "z_hi", 1)
    near = turned(ahead(lowered, "y"), y)
    distant = turned(ahead(across, "y"), y)
    all_lowered = turned([near, distant], z_hi)
    blended = (momentum.astype(f32) + gradient.astype(f32)).astype(bf16)
    half = blended.shape[0] // 2
    own_rows = lax.dynamic_slice_in_dim(blended, core * half, half, 0)
    other_rows = lax.dynamic_slice_in_dim(blended, (1 - core) * half, half, 0)

    sent = product(other_rows, all_lowered, 1, 1).astype(bf16)
    arrived = from_ahead(sent, "core", 1)
    partial_left = (product(own_rows, all_lowered, 1, 1) + arrived.astype(f32)).astype(bf16)
    pieces = lax.all_to_all(partial_left.reshape(FAR, -1, R), ("x", "z_lo"), 0, 0, tiled=True)
    left_rows = jnp.sum(pieces.astype(f32), axis=0).astype(bf16)
    own_left = from_everyone(left_rows, ("x", "z_lo")).reshape(half, R)
    other_left = from_ahead(own_left, "core", 1)
    left_factor = in_order(own_left, other_left, core)

    local_gram = product(left_factor, left_factor, 0, 0)
    packed = jnp.concatenate(
        [local_gram[i * BLOCK : (i + 1) * BLOCK, j * BLOCK : (j + 1) * BLOCK] for i, j in PAIRS]
    )
    piece = lax.dynamic_slice_in_dim(packed, (core * FAR + z_lo * 4 + x) * SHARE, SHARE, 0)
    over = from_ahead(piece, "z_hi", 1)
    gathered = [piece, over]
    for steps in range(1, 4):
        gathered.append(from_ahead(piece, "y", steps))
        gathered.append(from_diagonal(piece, steps))
    summed = sum(gathered[1:], gathered[0])
    line = jnp.concatenate(ahead(summed, "x"))
    own_gram = jnp.concatenate(ahead(line, "z_lo"))
    other_gram = from_ahead(own_gram, "core", 1)
    place = jnp.stack(
        [
            (core + c) % 2 * FAR + (z_lo + i) % 4 * 4 + (x + j) % 4
            for c in range(2)
            for i in range(4)
            for j in range(4)
        ]
    ).astype(jnp.int32)
    high, low = inverse_factor(place, own_gram, other_gram)

    partial_right = product(left_factor, blended, 0, 0).astype(bf16)
    quarter = R // 4
    parts = [
        lax.dynamic_slice_in_dim(partial_right, (y + steps) % 4 * quarter, quarter, 0) for steps in range(4)
    ]
    received = [parts[0]] + [from_ahead(parts[4 - steps], "y", steps) for steps in range(1, 4)]
    right_rows = sum(value.astype(f32) for value in received).astype(bf16)
    right_rows = (right_rows.astype(f32) + from_ahead(right_rows, "z_hi", 1).astype(f32)).astype(bf16)
    raw_right = turned(ahead(right_rows, "y"), y)

    right_factor = product(high, raw_right, 1, 0) + product(low, raw_right, 1, 0)
    square_sums = jnp.sum(from_everyone(jnp.sum(right_factor * right_factor, axis=1)[None], TENSOR), axis=(0, 1))
    orthonormal = (product(left_factor, high, 1, 1) + product(left_factor, low, 1, 1)).astype(bf16)
    inverse = lax.rsqrt(square_sums + epsilon)[:, None]
    full_factor = right_factor * inverse
    own_factor = lax.dynamic_slice_in_dim(full_factor, (z_hi * 4 + y) * columns, columns, 0).T
    taken = product(orthonormal, right_factor.astype(bf16), 1, 0)
    stepped = product(orthonormal, full_factor.astype(bf16), 1, 0)
    new_momentum = (blended.astype(f32) - (1.0 - decay_rate) * taken).astype(bf16)
    update = (stepped * jnp.sqrt(f32(D * FF / R))).astype(bf16)
    return (new_momentum, own_factor, update)


def solution(mesh):
    torus = Mesh(mesh.devices.reshape(2, 4, 4, 4, 2), ("z_hi", "y", "x", "z_lo", "core"))
    fsdp = ("z_hi", "y")
    return jax.shard_map(
        on_device,
        mesh=torus,
        in_specs=(P(fsdp, TENSOR), P(fsdp, TENSOR), P(TENSOR, fsdp)),
        out_specs=(P(fsdp, TENSOR), P(TENSOR, fsdp), P(fsdp, TENSOR)),
        check_vma=False,
    )
```

```python
import jax
import jax.numpy as jnp
from jax import lax
from jax.experimental import pallas as pl
from jax.experimental.pallas import tpu as pltpu
from jax.sharding import Mesh
from jax.sharding import PartitionSpec as P

D = 8192
FF = 28672
R = 512
FAR = 16
BLOCK = 128
BLOCKS = R // BLOCK
PAIRS = [(i, j) for i in range(BLOCKS) for j in range(i + 1)]
SHARE = len(PAIRS) * BLOCK // (2 * FAR)
SUB = 8
TENSOR = ("x", "z_lo", "core")

decay_rate = 0.95
epsilon = 1e-06
f32 = jnp.float32
bf16 = jnp.bfloat16


def product(left, right, left_dim, right_dim):
    return lax.dot_general(left, right, (((left_dim,), (right_dim,)), ((), ())), preferred_element_type=f32)


def added(terms):
    while len(terms) > 1:
        terms = [
            terms[i] + terms[i + 1] if i + 1 < len(terms) else terms[i] for i in range(0, len(terms), 2)
        ]
    return terms[0]


def spread(value):
    return jnp.broadcast_to(value, (SUB, BLOCK))


def small_inverse(entries):
    rest = [row[:] for row in entries]
    inverse = [None] * SUB
    upper = [[None] * SUB for _ in range(SUB)]
    for j in range(SUB):
        inverse[j] = lax.rsqrt(rest[j][j])
        for k in range(j + 1, SUB):
            upper[j][k] = rest[j][k] * inverse[j]
        for i in range(j + 1, SUB):
            for k in range(i, SUB):
                rest[i][k] = rest[i][k] - upper[j][i] * upper[j][k]
    result = [[None] * SUB for _ in range(SUB)]
    for j in range(SUB):
        result[j][j] = inverse[j]
        for i in range(j + 1, SUB):
            total = upper[j][i] * result[j][j]
            for k in range(j + 1, i):
                total = total + upper[k][i] * result[k][j]
            result[i][j] = -(inverse[i] * total)
    return result


def in_three(value):
    first = value.astype(bf16)
    rest = value - first.astype(f32)
    second = rest.astype(bf16)
    return first, second, (rest - second.astype(f32)).astype(bf16)


def exact(left, right, left_dim, right_dim):
    a, b, c = in_three(left)
    d, e, f = in_three(right)
    lefts = jnp.concatenate([a, a, b, b, a, c], axis=left_dim)
    rights = jnp.concatenate([d, e, d, e, f, d], axis=right_dim)
    return product(lefts, rights, left_dim, right_dim)


def factor_block(held):
    sub = lax.broadcasted_iota(jnp.int32, (SUB, BLOCK), 0)
    lane = lax.broadcasted_iota(jnp.int32, (SUB, BLOCK), 1)
    lane_row = lax.broadcasted_iota(jnp.int32, (1, BLOCK), 1)
    rows = held[0:SUB, :]
    for lo in range(0, BLOCK, SUB):
        hi = lo + SUB
        lanes = [spread(rows[:, lo + k : lo + k + 1]) for k in range(SUB)]
        entries = [[spread(lanes[k][i : i + 1, :]) if k >= i else None for k in range(SUB)] for i in range(SUB)]
        inverse = small_inverse(entries)
        columns = []
        for k in range(SUB):
            column = jnp.zeros((SUB, BLOCK), f32)
            for i in range(k, SUB):
                column = jnp.where(sub == i, inverse[i][k], column)
            columns.append(column)
        inside = (lane >= lo) & (lane < hi)
        rows = jnp.where(inside, jnp.where(lane - lo == sub, 1.0, 0.0), rows)
        done = added([columns[k] * spread(rows[k : k + 1, :]) for k in range(SUB)])
        held[lo:hi, :] = done
        if hi < BLOCK:
            following = held[hi : hi + SUB, :]
            across = [spread(following[:, lo + k : lo + k + 1]) for k in range(SUB)]
            weights = [added([across[k] * inverse[i][k] for k in range(i + 1)]) for i in range(SUB)]
            rows = jnp.where(inside, 0.0, following) - added(
                [weights[i] * spread(done[i : i + 1, :]) for i in range(SUB)]
            )
        if hi + SUB < BLOCK:
            change = exact(done, done, 0, 0)
            kept = jnp.where((lane_row >= lo) & (lane_row < hi), 0.0, held[hi + SUB :, :])
            held[hi + SUB :, :] = kept - change[hi + SUB :, :]


def inverse_kernel(place_ref, own_ref, other_ref, high_ref, low_ref, gram, inverse, held):
    first = {pair: n * BLOCK for n, pair in enumerate(PAIRS)}
    for n in range(2 * FAR):
        source = own_ref if n < FAR else other_ref
        into = pl.multiple_of(place_ref[n] * SHARE, SUB)
        gram[pl.ds(into, SHARE), :] = source[(n % FAR) * SHARE : (n % FAR + 1) * SHARE, :]

    def block(i, j):
        return gram[first[i, j] : first[i, j] + BLOCK, :]

    inverse[...] = jnp.zeros((R, R), f32)
    row = lax.broadcasted_iota(jnp.int32, (BLOCK, BLOCK), 0)
    column = lax.broadcasted_iota(jnp.int32, (BLOCK, BLOCK), 1)
    for b in range(BLOCKS):
        lo, hi = b * BLOCK, (b + 1) * BLOCK
        held[...] = block(b, b)
        factor_block(held)
        own = jnp.where(column <= row, held[...], 0.0)
        if b:
            inverse[lo:hi, :lo] = exact(own, inverse[lo:hi, :lo], 1, 0)
        inverse[lo:hi, lo:hi] = own
        lower = {i: exact(block(i, b), own, 1, 1) for i in range(b + 1, BLOCKS)}
        for i in range(b + 1, BLOCKS):
            for j in range(b + 1, i + 1):
                gram[first[i, j] : first[i, j] + BLOCK, :] = block(i, j) - exact(lower[i], lower[j], 1, 1)
            into = slice(i * BLOCK, (i + 1) * BLOCK)
            inverse[into, :hi] = inverse[into, :hi] - exact(lower[i], inverse[lo:hi, :hi], 1, 0)
    high = inverse[...].astype(bf16)
    high_ref[...] = high
    low_ref[...] = (inverse[...] - high.astype(f32)).astype(bf16)


def inverse_factor(place, own, other):
    whole = pl.BlockSpec(memory_space=pltpu.VMEM)
    return pl.pallas_call(
        inverse_kernel,
        out_shape=[jax.ShapeDtypeStruct((R, R), bf16)] * 2,
        in_specs=[pl.BlockSpec(memory_space=pltpu.SMEM), whole, whole],
        out_specs=[whole] * 2,
        scratch_shapes=[
            pltpu.VMEM((len(PAIRS) * BLOCK, BLOCK), f32),
            pltpu.VMEM((R, R), f32),
            pltpu.VMEM((BLOCK, BLOCK), f32),
        ],
        compiler_params=pltpu.CompilerParams(vmem_limit_bytes=32 << 20),
        cost_estimate=pl.CostEstimate(flops=2 * R**3, bytes_accessed=2 << 20, transcendentals=R),
    )(place, own, other)


def from_everyone(value, axis):
    length = lax.axis_size(axis)
    return lax.all_to_all(jnp.broadcast_to(value[None], (length, *value.shape)), axis, 0, 0, tiled=True)


def from_ahead(value, axis, steps):
    length = lax.axis_size(axis)
    return lax.ppermute(value, axis, [(i, (i - steps) % length) for i in range(length)])


def ahead(value, axis):
    return [value] + [from_ahead(value, axis, steps) for steps in range(1, lax.axis_size(axis))]


def in_order(own, other, core):
    first = jnp.where(core == 0, own, other)
    second = jnp.where(core == 0, other, own)
    return jnp.concatenate([first, second])


def on_device(momentum, gradient, factor):
    z_hi, y, x, z_lo, core = (lax.axis_index(name) for name in ("z_hi", "y", "x", "z_lo", "core"))
    columns = factor.shape[1]
    lowered = factor.T.astype(bf16)
    across = from_ahead(lowered, "z_hi", 1)
    both = jnp.stack([jnp.where(z_hi == 0, lowered, across), jnp.where(z_hi == 0, across, lowered)])
    all_lowered = jnp.moveaxis(from_everyone(both, "y"), 0, 1).reshape(R, -1)
    blended = (momentum.astype(f32) + gradient.astype(f32)).astype(bf16)
    half = blended.shape[0] // 2
    own_rows = lax.dynamic_slice_in_dim(blended, core * half, half, 0)
    other_rows = lax.dynamic_slice_in_dim(blended, (1 - core) * half, half, 0)

    sent = product(other_rows, all_lowered, 1, 1).astype(bf16)
    arrived = from_ahead(sent, "core", 1)
    partial_left = (product(own_rows, all_lowered, 1, 1) + arrived.astype(f32)).astype(bf16)
    pieces = lax.all_to_all(partial_left.reshape(FAR, -1, R), ("x", "z_lo"), 0, 0, tiled=True)
    left_rows = jnp.sum(pieces.astype(f32), axis=0).astype(bf16)
    own_left = from_everyone(left_rows, ("x", "z_lo")).reshape(half, R)
    other_left = from_ahead(own_left, "core", 1)
    left_factor = in_order(own_left, other_left, core)

    partial_right = product(left_factor, blended, 0, 0).astype(bf16)
    received = lax.all_to_all(partial_right.reshape(8, columns, -1), ("z_hi", "y"), 0, 0, tiled=True)

    gram_left, _ = lax.optimization_barrier((left_factor, partial_right))
    local_gram = product(gram_left, gram_left, 0, 0)
    packed = jnp.concatenate(
        [local_gram[i * BLOCK : (i + 1) * BLOCK, j * BLOCK : (j + 1) * BLOCK] for i, j in PAIRS]
    )
    piece = lax.dynamic_slice_in_dim(packed, (core * FAR + z_lo * 4 + x) * SHARE, SHARE, 0)
    along = ahead(piece, "y")
    summed = sum(along[1:], along[0])
    summed = summed + from_ahead(summed, "z_hi", 1)
    line = jnp.concatenate(ahead(summed, "x"))
    received, line = lax.optimization_barrier((received, line))
    right_rows = jnp.sum(received.astype(f32), axis=0).astype(bf16)
    raw_right = from_everyone(right_rows, ("z_hi", "y")).reshape(R, -1)
    line, _ = lax.optimization_barrier((line, right_rows))
    own_gram = jnp.concatenate(ahead(line, "z_lo"))
    other_gram = from_ahead(own_gram, "core", 1)
    place = jnp.stack(
        [
            (core + c) % 2 * FAR + (z_lo + i) % 4 * 4 + (x + j) % 4
            for c in range(2)
            for i in range(4)
            for j in range(4)
        ]
    ).astype(jnp.int32)
    high, low = inverse_factor(place, own_gram, other_gram)

    right_factor = product(high, raw_right, 1, 0) + product(low, raw_right, 1, 0)
    square_sums = jnp.sum(from_everyone(jnp.sum(right_factor * right_factor, axis=1)[None], TENSOR), axis=(0, 1))
    orthonormal = (product(left_factor, high, 1, 1) + product(left_factor, low, 1, 1)).astype(bf16)
    inverse = lax.rsqrt(square_sums + epsilon)[:, None]
    full_factor = right_factor * inverse
    own_factor = lax.dynamic_slice_in_dim(full_factor, (z_hi * 4 + y) * columns, columns, 0).T
    taken = product(orthonormal, right_factor.astype(bf16), 1, 0)
    stepped = product(orthonormal, full_factor.astype(bf16), 1, 0)
    new_momentum = (blended.astype(f32) - (1.0 - decay_rate) * taken).astype(bf16)
    update = (stepped * jnp.sqrt(f32(D * FF / R))).astype(bf16)
    return (new_momentum, own_factor, update)


def solution(mesh):
    torus = Mesh(mesh.devices.reshape(2, 4, 4, 4, 2), ("z_hi", "y", "x", "z_lo", "core"))
    fsdp = ("z_hi", "y")
    return jax.shard_map(
        on_device,
        mesh=torus,
        in_specs=(P(fsdp, TENSOR), P(fsdp, TENSOR), P(TENSOR, fsdp)),
        out_specs=(P(fsdp, TENSOR), P(TENSOR, fsdp), P(fsdp, TENSOR)),
        check_vma=False,
    )
```

```python
import jax
import jax.numpy as jnp
from jax import lax
from jax.experimental import pallas as pl
from jax.experimental.pallas import tpu as pltpu
from jax.sharding import Mesh
from jax.sharding import PartitionSpec as P

D = 8192
FF = 28672
R = 512
FAR = 16
BLOCK = 128
BLOCKS = R // BLOCK
PAIRS = [(i, j) for i in range(BLOCKS) for j in range(i + 1)]
SHARE = len(PAIRS) * BLOCK // (2 * FAR)
SUB = 8
HALF = BLOCKS // 2
LATER = [(i, j) for i, j in PAIRS if j >= HALF]
TENSOR = ("x", "z_lo", "core")

decay_rate = 0.95
epsilon = 1e-06
f32 = jnp.float32
bf16 = jnp.bfloat16


def product(left, right, left_dim, right_dim):
    return lax.dot_general(left, right, (((left_dim,), (right_dim,)), ((), ())), preferred_element_type=f32)


def added(terms):
    while len(terms) > 1:
        terms = [
            terms[i] + terms[i + 1] if i + 1 < len(terms) else terms[i] for i in range(0, len(terms), 2)
        ]
    return terms[0]


def spread(value):
    return jnp.broadcast_to(value, (SUB, BLOCK))


def small_inverse(entries):
    rest = [row[:] for row in entries]
    inverse = [None] * SUB
    upper = [[None] * SUB for _ in range(SUB)]
    for j in range(SUB):
        inverse[j] = lax.rsqrt(rest[j][j])
        for k in range(j + 1, SUB):
            upper[j][k] = rest[j][k] * inverse[j]
        for i in range(j + 1, SUB):
            for k in range(i, SUB):
                rest[i][k] = rest[i][k] - upper[j][i] * upper[j][k]
    result = [[None] * SUB for _ in range(SUB)]
    for j in range(SUB):
        result[j][j] = inverse[j]
        for i in range(j + 1, SUB):
            total = upper[j][i] * result[j][j]
            for k in range(j + 1, i):
                total = total + upper[k][i] * result[k][j]
            result[i][j] = -(inverse[i] * total)
    return result


def in_three(value):
    first = value.astype(bf16)
    rest = value - first.astype(f32)
    second = rest.astype(bf16)
    return first, second, (rest - second.astype(f32)).astype(bf16)


def exact(left, right, left_dim, right_dim):
    a, b, c = in_three(left)
    d, e, f = in_three(right)
    lefts = jnp.concatenate([a, a, b, b, a, c], axis=left_dim)
    rights = jnp.concatenate([d, e, d, e, f, d], axis=right_dim)
    return product(lefts, rights, left_dim, right_dim)


def factor_block(held):
    sub = lax.broadcasted_iota(jnp.int32, (SUB, BLOCK), 0)
    lane = lax.broadcasted_iota(jnp.int32, (SUB, BLOCK), 1)
    lane_row = lax.broadcasted_iota(jnp.int32, (1, BLOCK), 1)
    rows = held[0:SUB, :]
    for lo in range(0, BLOCK, SUB):
        hi = lo + SUB
        lanes = [spread(rows[:, lo + k : lo + k + 1]) for k in range(SUB)]
        entries = [[spread(lanes[k][i : i + 1, :]) if k >= i else None for k in range(SUB)] for i in range(SUB)]
        inverse = small_inverse(entries)
        columns = []
        for k in range(SUB):
            column = jnp.zeros((SUB, BLOCK), f32)
            for i in range(k, SUB):
                column = jnp.where(sub == i, inverse[i][k], column)
            columns.append(column)
        inside = (lane >= lo) & (lane < hi)
        rows = jnp.where(inside, jnp.where(lane - lo == sub, 1.0, 0.0), rows)
        done = added([columns[k] * spread(rows[k : k + 1, :]) for k in range(SUB)])
        held[lo:hi, :] = done
        if hi < BLOCK:
            following = held[hi : hi + SUB, :]
            across = [spread(following[:, lo + k : lo + k + 1]) for k in range(SUB)]
            weights = [added([across[k] * inverse[i][k] for k in range(i + 1)]) for i in range(SUB)]
            rows = jnp.where(inside, 0.0, following) - added(
                [weights[i] * spread(done[i : i + 1, :]) for i in range(SUB)]
            )
        if hi + SUB < BLOCK:
            change = exact(done, done, 0, 0)
            kept = jnp.where((lane_row >= lo) & (lane_row < hi), 0.0, held[hi + SUB :, :])
            held[hi + SUB :, :] = kept - change[hi + SUB :, :]


FIRST = {pair: n * BLOCK for n, pair in enumerate(PAIRS)}


def eliminate(b, stored, gram, inverse, held):
    row = lax.broadcasted_iota(jnp.int32, (BLOCK, BLOCK), 0)
    column = lax.broadcasted_iota(jnp.int32, (BLOCK, BLOCK), 1)

    def block(i, j):
        return gram[stored[i, j] : stored[i, j] + BLOCK, :]

    lo, hi = b * BLOCK, (b + 1) * BLOCK
    held[...] = block(b, b)
    factor_block(held)
    own = jnp.where(column <= row, held[...], 0.0)
    if b:
        inverse[lo:hi, :lo] = exact(own, inverse[lo:hi, :lo], 1, 0)
    inverse[lo:hi, lo:hi] = own
    lower = {i: exact(block(i, b), own, 1, 1) for i in range(b + 1, BLOCKS)}
    for i in range(b + 1, BLOCKS):
        for j in range(b + 1, i + 1):
            gram[stored[i, j] : stored[i, j] + BLOCK, :] = block(i, j) - exact(lower[i], lower[j], 1, 1)
        into = slice(i * BLOCK, (i + 1) * BLOCK)
        inverse[into, :hi] = inverse[into, :hi] - exact(lower[i], inverse[lo:hi, :hi], 1, 0)


def first_kernel(place_ref, own_ref, other_ref, rest_ref, inverse, gram, held):
    for n in range(2 * FAR):
        source = own_ref if n < FAR else other_ref
        into = pl.multiple_of(place_ref[n] * SHARE, SUB)
        gram[pl.ds(into, SHARE), :] = source[(n % FAR) * SHARE : (n % FAR + 1) * SHARE, :]
    inverse[...] = jnp.zeros_like(inverse)
    for b in range(HALF):
        eliminate(b, FIRST, gram, inverse, held)
    for n, pair in enumerate(LATER):
        rest_ref[n * BLOCK : (n + 1) * BLOCK, :] = gram[FIRST[pair] : FIRST[pair] + BLOCK, :]


def second_kernel(rest_ref, begun_ref, high_ref, low_ref, inverse, gram, held):
    gram[...] = rest_ref[...]
    inverse[:, : HALF * BLOCK] = begun_ref[...]
    inverse[:, HALF * BLOCK :] = jnp.zeros((R, R - HALF * BLOCK), f32)
    stored = {pair: n * BLOCK for n, pair in enumerate(LATER)}
    for b in range(HALF, BLOCKS):
        eliminate(b, stored, gram, inverse, held)
    high = inverse[...].astype(bf16)
    high_ref[...] = high
    low_ref[...] = (inverse[...] - high.astype(f32)).astype(bf16)


def block_call(kernel, inputs, outputs, scratch):
    whole = pl.BlockSpec(memory_space=pltpu.VMEM)
    small = pl.BlockSpec(memory_space=pltpu.SMEM)
    return pl.pallas_call(
        kernel,
        out_shape=[jax.ShapeDtypeStruct(shape, dtype) for shape, dtype in outputs],
        in_specs=[whole if value.dtype == f32 else small for value in inputs],
        out_specs=[whole] * len(outputs),
        scratch_shapes=[pltpu.VMEM(shape, f32) for shape in scratch],
        compiler_params=pltpu.CompilerParams(vmem_limit_bytes=32 << 20),
        cost_estimate=pl.CostEstimate(flops=10 * R**3, bytes_accessed=2 << 20, transcendentals=R),
    )(*inputs)


def from_everyone(value, axis):
    length = lax.axis_size(axis)
    return lax.all_to_all(jnp.broadcast_to(value[None], (length, *value.shape)), axis, 0, 0, tiled=True)


def from_ahead(value, axis, steps):
    length = lax.axis_size(axis)
    return lax.ppermute(value, axis, [(i, (i - steps) % length) for i in range(length)])


def ahead(value, axis):
    return [value] + [from_ahead(value, axis, steps) for steps in range(1, lax.axis_size(axis))]


def in_order(own, other, core):
    first = jnp.where(core == 0, own, other)
    second = jnp.where(core == 0, other, own)
    return jnp.concatenate([first, second])


def on_device(momentum, gradient, factor):
    z_hi, y, x, z_lo, core = (lax.axis_index(name) for name in ("z_hi", "y", "x", "z_lo", "core"))
    columns = factor.shape[1]
    lowered = factor.T.astype(bf16)
    across = from_ahead(lowered, "z_hi", 1)
    both = jnp.stack([jnp.where(z_hi == 0, lowered, across), jnp.where(z_hi == 0, across, lowered)])
    all_lowered = jnp.moveaxis(from_everyone(both, "y"), 0, 1).reshape(R, -1)
    blended = (momentum.astype(f32) + gradient.astype(f32)).astype(bf16)
    half = blended.shape[0] // 2
    own_rows = lax.dynamic_slice_in_dim(blended, core * half, half, 0)
    other_rows = lax.dynamic_slice_in_dim(blended, (1 - core) * half, half, 0)

    sent = product(other_rows, all_lowered, 1, 1).astype(bf16)
    arrived = from_ahead(sent, "core", 1)
    partial_left = (product(own_rows, all_lowered, 1, 1) + arrived.astype(f32)).astype(bf16)
    pieces = lax.all_to_all(partial_left.reshape(FAR, -1, R), ("x", "z_lo"), 0, 0, tiled=True)
    left_rows = jnp.sum(pieces.astype(f32), axis=0).astype(bf16)
    own_left = from_everyone(left_rows, ("x", "z_lo")).reshape(half, R)
    other_left = from_ahead(own_left, "core", 1)
    left_factor = in_order(own_left, other_left, core)

    local_gram = product(left_factor, left_factor, 0, 0)
    packed = jnp.concatenate(
        [local_gram[i * BLOCK : (i + 1) * BLOCK, j * BLOCK : (j + 1) * BLOCK] for i, j in PAIRS]
    )
    piece = lax.dynamic_slice_in_dim(packed, (core * FAR + z_lo * 4 + x) * SHARE, SHARE, 0)
    summed = jnp.sum(from_everyone(piece, ("z_hi", "y")), axis=0)

    partial_right = product(left_factor, blended, 0, 0).astype(bf16)
    summed, partial_right = lax.optimization_barrier((summed, partial_right))
    received = lax.all_to_all(partial_right.reshape(4, R // 4, -1), "y", 0, 0, tiled=True)

    line = jnp.concatenate(ahead(summed, "x"))
    own_gram = jnp.concatenate(ahead(line, "z_lo"))
    other_gram = from_ahead(own_gram, "core", 1)
    place = jnp.stack(
        [
            (core + c) % 2 * FAR + (z_lo + i) % 4 * 4 + (x + j) % 4
            for c in range(2)
            for i in range(4)
            for j in range(4)
        ]
    ).astype(jnp.int32)

    received, other_gram = lax.optimization_barrier((received, other_gram))
    right_rows = jnp.sum(received.astype(f32), axis=0).astype(bf16)
    other_gram, right_rows = lax.optimization_barrier((other_gram, right_rows))
    opposite = from_ahead(right_rows, "z_hi", 1)
    rest, begun = block_call(
        first_kernel,
        (place, own_gram, other_gram),
        [((len(LATER) * BLOCK, BLOCK), f32), ((R, HALF * BLOCK), f32)],
        [(len(PAIRS) * BLOCK, BLOCK), (BLOCK, BLOCK)],
    )
    opposite, rest = lax.optimization_barrier((opposite, rest))
    right_rows = (right_rows.astype(f32) + opposite.astype(f32)).astype(bf16)
    rest, right_rows = lax.optimization_barrier((rest, right_rows))
    raw_right = from_everyone(right_rows, "y").reshape(R, -1)
    high, low = block_call(
        second_kernel,
        (rest, begun),
        [((R, R), bf16)] * 2,
        [(R, R), (len(LATER) * BLOCK, BLOCK), (BLOCK, BLOCK)],
    )

    right_factor = product(high, raw_right, 1, 0) + product(low, raw_right, 1, 0)
    own_sums = jnp.sum(right_factor * right_factor, axis=1)[None]
    last_left, own_sums = lax.optimization_barrier((left_factor, own_sums))
    square_sums = jnp.sum(from_everyone(own_sums, TENSOR), axis=(0, 1))
    orthonormal = (product(last_left, high, 1, 1) + product(last_left, low, 1, 1)).astype(bf16)
    inverse = lax.rsqrt(square_sums + epsilon)[:, None]
    full_factor = right_factor * inverse
    own_factor = lax.dynamic_slice_in_dim(full_factor, (z_hi * 4 + y) * columns, columns, 0).T
    taken = product(orthonormal, right_factor.astype(bf16), 1, 0)
    stepped = product(orthonormal, full_factor.astype(bf16), 1, 0)
    new_momentum = (blended.astype(f32) - (1.0 - decay_rate) * taken).astype(bf16)
    update = (stepped * jnp.sqrt(f32(D * FF / R))).astype(bf16)
    return (new_momentum, own_factor, update)


def solution(mesh):
    torus = Mesh(mesh.devices.reshape(2, 4, 4, 4, 2), ("z_hi", "y", "x", "z_lo", "core"))
    fsdp = ("z_hi", "y")
    return jax.shard_map(
        on_device,
        mesh=torus,
        in_specs=(P(fsdp, TENSOR), P(fsdp, TENSOR), P(TENSOR, fsdp)),
        out_specs=(P(fsdp, TENSOR), P(TENSOR, fsdp), P(fsdp, TENSOR)),
        check_vma=False,
    )
```

```python
import jax
import jax.numpy as jnp
from jax import lax
from jax.experimental import pallas as pl
from jax.experimental.pallas import tpu as pltpu
from jax.sharding import Mesh
from jax.sharding import PartitionSpec as P

D = 8192
FF = 28672
R = 512
FAR = 16
BLOCK = 128
BLOCKS = R // BLOCK
PAIRS = [(i, j) for i in range(BLOCKS) for j in range(i + 1)]
SHARE = len(PAIRS) * BLOCK // (2 * FAR)
SUB = 8
TENSOR = ("x", "z_lo", "core")

decay_rate = 0.95
epsilon = 1e-06
f32 = jnp.float32
bf16 = jnp.bfloat16


def product(left, right, left_dim, right_dim):
    return lax.dot_general(left, right, (((left_dim,), (right_dim,)), ((), ())), preferred_element_type=f32)


def added(terms):
    while len(terms) > 1:
        terms = [
            terms[i] + terms[i + 1] if i + 1 < len(terms) else terms[i] for i in range(0, len(terms), 2)
        ]
    return terms[0]


def spread(value):
    return jnp.broadcast_to(value, (SUB, BLOCK))


def small_inverse(entries):
    rest = [row[:] for row in entries]
    inverse = [None] * SUB
    upper = [[None] * SUB for _ in range(SUB)]
    for j in range(SUB):
        inverse[j] = lax.rsqrt(rest[j][j])
        for k in range(j + 1, SUB):
            upper[j][k] = rest[j][k] * inverse[j]
        for i in range(j + 1, SUB):
            for k in range(i, SUB):
                rest[i][k] = rest[i][k] - upper[j][i] * upper[j][k]
    result = [[None] * SUB for _ in range(SUB)]
    for j in range(SUB):
        result[j][j] = inverse[j]
        for i in range(j + 1, SUB):
            total = upper[j][i] * result[j][j]
            for k in range(j + 1, i):
                total = total + upper[k][i] * result[k][j]
            result[i][j] = -(inverse[i] * total)
    return result


def in_three(value):
    first = value.astype(bf16)
    rest = value - first.astype(f32)
    second = rest.astype(bf16)
    return first, second, (rest - second.astype(f32)).astype(bf16)


def exact(left, right, left_dim, right_dim):
    a, b, c = in_three(left)
    d, e, f = in_three(right)
    lefts = jnp.concatenate([a, a, b, b, a, c], axis=left_dim)
    rights = jnp.concatenate([d, e, d, e, f, d], axis=right_dim)
    return product(lefts, rights, left_dim, right_dim)


def factor_block(held):
    sub = lax.broadcasted_iota(jnp.int32, (SUB, BLOCK), 0)
    lane = lax.broadcasted_iota(jnp.int32, (SUB, BLOCK), 1)
    lane_row = lax.broadcasted_iota(jnp.int32, (1, BLOCK), 1)
    rows = held[0:SUB, :]
    for lo in range(0, BLOCK, SUB):
        hi = lo + SUB
        lanes = [spread(rows[:, lo + k : lo + k + 1]) for k in range(SUB)]
        entries = [[spread(lanes[k][i : i + 1, :]) if k >= i else None for k in range(SUB)] for i in range(SUB)]
        inverse = small_inverse(entries)
        columns = []
        for k in range(SUB):
            column = jnp.zeros((SUB, BLOCK), f32)
            for i in range(k, SUB):
                column = jnp.where(sub == i, inverse[i][k], column)
            columns.append(column)
        inside = (lane >= lo) & (lane < hi)
        rows = jnp.where(inside, jnp.where(lane - lo == sub, 1.0, 0.0), rows)
        done = added([columns[k] * spread(rows[k : k + 1, :]) for k in range(SUB)])
        held[lo:hi, :] = done
        if hi < BLOCK:
            following = held[hi : hi + SUB, :]
            across = [spread(following[:, lo + k : lo + k + 1]) for k in range(SUB)]
            weights = [added([across[k] * inverse[i][k] for k in range(i + 1)]) for i in range(SUB)]
            rows = jnp.where(inside, 0.0, following) - added(
                [weights[i] * spread(done[i : i + 1, :]) for i in range(SUB)]
            )
        if hi + SUB < BLOCK:
            change = exact(done, done, 0, 0)
            kept = jnp.where((lane_row >= lo) & (lane_row < hi), 0.0, held[hi + SUB :, :])
            held[hi + SUB :, :] = kept - change[hi + SUB :, :]


FIRST = {pair: n * BLOCK for n, pair in enumerate(PAIRS)}


def eliminate(b, gram, inverse, held):
    row = lax.broadcasted_iota(jnp.int32, (BLOCK, BLOCK), 0)
    column = lax.broadcasted_iota(jnp.int32, (BLOCK, BLOCK), 1)

    def block(i, j):
        return gram[FIRST[i, j] : FIRST[i, j] + BLOCK, :]

    lo, hi = b * BLOCK, (b + 1) * BLOCK
    held[...] = block(b, b)
    factor_block(held)
    own = jnp.where(column <= row, held[...], 0.0)
    if b:
        inverse[lo:hi, :lo] = exact(own, inverse[lo:hi, :lo], 1, 0)
    inverse[lo:hi, lo:hi] = own
    lower = {i: exact(block(i, b), own, 1, 1) for i in range(b + 1, BLOCKS)}
    for i in range(b + 1, BLOCKS):
        for j in range(b + 1, i + 1):
            gram[FIRST[i, j] : FIRST[i, j] + BLOCK, :] = block(i, j) - exact(lower[i], lower[j], 1, 1)
        into = slice(i * BLOCK, (i + 1) * BLOCK)
        inverse[into, :hi] = inverse[into, :hi] - exact(lower[i], inverse[lo:hi, :hi], 1, 0)


def inverse_kernel(place_ref, own_ref, other_ref, high_ref, low_ref, gram, inverse, held):
    for n in range(2 * FAR):
        source = own_ref if n < FAR else other_ref
        into = pl.multiple_of(place_ref[n] * SHARE, SUB)
        gram[pl.ds(into, SHARE), :] = source[(n % FAR) * SHARE : (n % FAR + 1) * SHARE, :]
    inverse[...] = jnp.zeros_like(inverse)
    for b in range(BLOCKS):
        eliminate(b, gram, inverse, held)
    high = inverse[...].astype(bf16)
    high_ref[...] = high
    low_ref[...] = (inverse[...] - high.astype(f32)).astype(bf16)


def kernel_call(kernel, place, inputs, outputs, scratch, flops):
    whole = pl.BlockSpec(memory_space=pltpu.VMEM)
    return pl.pallas_call(
        kernel,
        out_shape=outputs,
        in_specs=[pl.BlockSpec(memory_space=pltpu.SMEM)] + [whole] * len(inputs),
        out_specs=[whole] * len(outputs),
        scratch_shapes=[pltpu.VMEM(shape, f32) for shape in scratch],
        compiler_params=pltpu.CompilerParams(vmem_limit_bytes=32 << 20),
        cost_estimate=pl.CostEstimate(flops=flops, bytes_accessed=2 << 20, transcendentals=0),
    )(place, *inputs)


def inverse_factor(place, own, other):
    return kernel_call(
        inverse_kernel,
        place,
        (own, other),
        [jax.ShapeDtypeStruct((R, R), bf16)] * 2,
        [(len(PAIRS) * BLOCK, BLOCK), (R, R), (BLOCK, BLOCK)],
        20 * R**3,
    )


def arrange(place, inputs, rows):
    def kernel(place_ref, *refs):
        n = 0
        for source in refs[:-1]:
            for lo in range(0, source.shape[0], rows):
                into = pl.multiple_of(place_ref[n] * rows, rows)
                refs[-1][pl.ds(into, rows), :] = source[lo : lo + rows, :]
                n += 1

    height = sum(value.shape[0] for value in inputs)
    output = jax.ShapeDtypeStruct((height, inputs[0].shape[1]), inputs[0].dtype)
    return kernel_call(kernel, place, inputs, [output], [], 1 << 20)[0]


def from_everyone(value, axis):
    length = lax.axis_size(axis)
    return lax.all_to_all(jnp.broadcast_to(value[None], (length, *value.shape)), axis, 0, 0, tiled=True)


def from_ahead(value, axis, steps):
    length = lax.axis_size(axis)
    return lax.ppermute(value, axis, [(i, (i - steps) % length) for i in range(length)])


def ahead(value, axis):
    return [value] + [from_ahead(value, axis, steps) for steps in range(1, lax.axis_size(axis))]


def exchanged(value, axis, index):
    count = lax.axis_size(axis)
    length = value.shape[0] // count
    pieces = [lax.dynamic_slice_in_dim(value, (index + k) % count * length, length, 0) for k in range(count)]
    return [pieces[0]] + [from_ahead(pieces[count - k], axis, k) for k in range(1, count)]


def total(pieces):
    return sum((value.astype(f32) for value in pieces[1:]), pieces[0].astype(f32))


def on_device(momentum, gradient, factor):
    z_hi, y, x, z_lo, core = (lax.axis_index(name) for name in ("z_hi", "y", "x", "z_lo", "core"))
    columns = factor.shape[1]
    tensor_place = jnp.stack(
        [
            (core + c) % 2 * FAR + (x + j) % 4 * 4 + (z_lo + i) % 4
            for c in range(2)
            for j in range(4)
            for i in range(4)
        ]
    ).astype(jnp.int32)
    fsdp_place = jnp.stack([(z_hi + h) % 2 * 4 + (y + k) % 4 for h in range(2) for k in range(4)]).astype(jnp.int32)
    y_place = jnp.stack([(y + k) % 4 for k in range(4)]).astype(jnp.int32)

    lowered = factor.T.astype(bf16)
    near = ahead(lowered, "y")
    across = ahead(from_ahead(lowered, "z_hi", 1), "y")
    all_lowered = arrange(fsdp_place, near + across, columns)
    blended = (momentum.astype(f32) + gradient.astype(f32)).astype(bf16)
    half = blended.shape[0] // 2
    own_rows = lax.dynamic_slice_in_dim(blended, core * half, half, 0)
    other_rows = lax.dynamic_slice_in_dim(blended, (1 - core) * half, half, 0)

    sent = product(other_rows, all_lowered, 1, 1).astype(bf16)
    arrived = from_ahead(sent, "core", 1)
    partial_left = (product(own_rows, all_lowered, 1, 1) + arrived.astype(f32)).astype(bf16)
    left_line = total(exchanged(partial_left, "x", x)).astype(bf16)
    left_rows = total(exchanged(left_line, "z_lo", z_lo)).astype(bf16)
    left_line = jnp.concatenate(ahead(left_rows, "z_lo"))
    own_left = jnp.concatenate(ahead(left_line, "x"))
    other_left = from_ahead(own_left, "core", 1)

    local_gram = product(own_left, own_left, 0, 0) + product(other_left, other_left, 0, 0)
    packed = jnp.concatenate(
        [local_gram[i * BLOCK : (i + 1) * BLOCK, j * BLOCK : (j + 1) * BLOCK] for i, j in PAIRS]
    )
    piece = lax.dynamic_slice_in_dim(packed, (core * FAR + x * 4 + z_lo) * SHARE, SHARE, 0)
    summed = jnp.sum(from_everyone(piece, ("z_hi", "y")), axis=0)

    left_factor = arrange(tensor_place, (own_left, other_left), half // FAR)
    partial_right = product(left_factor, blended, 0, 0).astype(bf16)
    received = exchanged(partial_right, "y", y)

    gram_line = jnp.concatenate(ahead(summed, "z_lo"))
    gram_line, *received = lax.optimization_barrier((gram_line, *received))
    right_rows = total(received).astype(bf16)
    gram_line, right_rows = lax.optimization_barrier((gram_line, right_rows))
    opposite = from_ahead(right_rows, "z_hi", 1)
    opposite, *gram_lines = lax.optimization_barrier((opposite, *ahead(gram_line, "x")))
    own_gram = jnp.concatenate(gram_lines)
    other_gram = from_ahead(own_gram, "core", 1)
    right_rows = total([right_rows, opposite]).astype(bf16)
    other_gram, right_rows = lax.optimization_barrier((other_gram, right_rows))
    right_pieces = ahead(right_rows, "y")
    high, low = inverse_factor(tensor_place, own_gram, other_gram)
    raw_right = arrange(y_place, right_pieces, R // 4)

    right_factor = product(high, raw_right, 1, 0) + product(low, raw_right, 1, 0)
    own_sums = jnp.sum(right_factor * right_factor, axis=1)[None]
    last_left, own_sums = lax.optimization_barrier((left_factor, own_sums))
    square_sums = jnp.sum(from_everyone(own_sums, TENSOR), axis=(0, 1))
    orthonormal = (product(last_left, high, 1, 1) + product(last_left, low, 1, 1)).astype(bf16)
    inverse = lax.rsqrt(square_sums + epsilon)[:, None]
    full_factor = right_factor * inverse
    own_factor = lax.dynamic_slice_in_dim(full_factor, (z_hi * 4 + y) * columns, columns, 0).T
    taken = product(orthonormal, right_factor.astype(bf16), 1, 0)
    stepped = product(orthonormal, full_factor.astype(bf16), 1, 0)
    new_momentum = (blended.astype(f32) - (1.0 - decay_rate) * taken).astype(bf16)
    update = (stepped * jnp.sqrt(f32(D * FF / R))).astype(bf16)
    return (new_momentum, own_factor, update)


def solution(mesh):
    torus = Mesh(mesh.devices.reshape(2, 4, 4, 4, 2), ("z_hi", "y", "x", "z_lo", "core"))
    fsdp = ("z_hi", "y")
    return jax.shard_map(
        on_device,
        mesh=torus,
        in_specs=(P(fsdp, TENSOR), P(fsdp, TENSOR), P(TENSOR, fsdp)),
        out_specs=(P(fsdp, TENSOR), P(TENSOR, fsdp), P(fsdp, TENSOR)),
        check_vma=False,
    )
```

```python
import math

import jax
import jax.numpy as jnp
from jax import lax
from jax.experimental import pallas as pl
from jax.experimental.pallas import tpu as pltpu
from jax.sharding import Mesh
from jax.sharding import PartitionSpec as P

D = 8192
FF = 28672
R = 512
FAR = 16
BLOCK = 128
BLOCKS = R // BLOCK
PAIRS = [(i, j) for i in range(BLOCKS) for j in range(i + 1)]
SHARE = len(PAIRS) * BLOCK // (2 * FAR)
SUB = 8
TENSOR = ("x", "z_lo", "core")

decay_rate = 0.95
epsilon = 1e-06
f32 = jnp.float32
bf16 = jnp.bfloat16


def product(left, right, left_dim, right_dim):
    return lax.dot_general(left, right, (((left_dim,), (right_dim,)), ((), ())), preferred_element_type=f32)


def added(terms):
    while len(terms) > 1:
        terms = [
            terms[i] + terms[i + 1] if i + 1 < len(terms) else terms[i] for i in range(0, len(terms), 2)
        ]
    return terms[0]


def spread(value):
    return jnp.broadcast_to(value, (SUB, BLOCK))


def small_inverse(entries):
    rest = [row[:] for row in entries]
    inverse = [None] * SUB
    upper = [[None] * SUB for _ in range(SUB)]
    for j in range(SUB):
        inverse[j] = lax.rsqrt(rest[j][j])
        for k in range(j + 1, SUB):
            upper[j][k] = rest[j][k] * inverse[j]
        for i in range(j + 1, SUB):
            for k in range(i, SUB):
                rest[i][k] = rest[i][k] - upper[j][i] * upper[j][k]
    result = [[None] * SUB for _ in range(SUB)]
    for j in range(SUB):
        result[j][j] = inverse[j]
        for i in range(j + 1, SUB):
            total = upper[j][i] * result[j][j]
            for k in range(j + 1, i):
                total = total + upper[k][i] * result[k][j]
            result[i][j] = -(inverse[i] * total)
    return result


def in_three(value):
    first = value.astype(bf16)
    rest = value - first.astype(f32)
    second = rest.astype(bf16)
    return first, second, (rest - second.astype(f32)).astype(bf16)


def exact(left, right, left_dim, right_dim):
    a, b, c = in_three(left)
    d, e, f = in_three(right)
    lefts = jnp.concatenate([a, a, b, b, a, c], axis=left_dim)
    rights = jnp.concatenate([d, e, d, e, f, d], axis=right_dim)
    return product(lefts, rights, left_dim, right_dim)


def factor_block(held):
    sub = lax.broadcasted_iota(jnp.int32, (SUB, BLOCK), 0)
    lane = lax.broadcasted_iota(jnp.int32, (SUB, BLOCK), 1)
    lane_row = lax.broadcasted_iota(jnp.int32, (1, BLOCK), 1)
    rows, following = held[:SUB, :], held[SUB : 2 * SUB, :]
    for lo in range(0, BLOCK, SUB):
        inside = (lane >= lo) & (lane < lo + SUB)
        lanes = [spread(rows[:, lo + k : lo + k + 1]) for k in range(SUB)]
        entries = [[spread(lanes[k][i : i + 1, :]) if k >= i else None for k in range(SUB)] for i in range(SUB)]
        inverse = small_inverse(entries)
        bare = [
            jnp.where(lane == lo + k, 1.0, jnp.where(inside, 0.0, spread(rows[k : k + 1, :]))) for k in range(SUB)
        ]
        done = [added([inverse[i][k] * bare[k] for k in range(i + 1)]) for i in range(SUB)]
        packed = done[0]
        for i in range(1, SUB):
            packed = jnp.where(sub == i, done[i], packed)
        held[lo : lo + SUB, :] = packed
        if lo + SUB < BLOCK:
            weights = [added([inverse[m][k] * done[m] for m in range(k, SUB)]) for k in range(SUB)]

            def brought(later):
                terms = [spread(later[:, lo + k : lo + k + 1]) * weights[k] for k in range(SUB)]
                return jnp.where(inside, 0.0, later) - added(terms)

            rows = brought(following)
        if lo + 2 * SUB < BLOCK:
            following = brought(held[lo + 2 * SUB : lo + 3 * SUB, :])
        if lo + 3 * SUB < BLOCK:
            change = exact(packed, packed, 0, 0)
            kept = jnp.where((lane_row >= lo) & (lane_row < lo + SUB), 0.0, held[lo + 3 * SUB :, :])
            held[lo + 3 * SUB :, :] = kept - change[lo + 3 * SUB :, :]


FIRST = {pair: n * BLOCK for n, pair in enumerate(PAIRS)}


def eliminate(b, own, gram, inverse):
    def block(i, j):
        return gram[FIRST[i, j] : FIRST[i, j] + BLOCK, :]

    lo, hi = b * BLOCK, (b + 1) * BLOCK
    if b:
        inverse[lo:hi, :lo] = exact(own, inverse[lo:hi, :lo], 1, 0)
    inverse[lo:hi, lo:hi] = own
    lower = {i: exact(block(i, b), own, 1, 1) for i in range(b + 1, BLOCKS)}
    for i in range(b + 1, BLOCKS):
        for j in range(b + 1, i + 1):
            gram[FIRST[i, j] : FIRST[i, j] + BLOCK, :] = block(i, j) - exact(lower[i], lower[j], 1, 1)
        into = slice(i * BLOCK, (i + 1) * BLOCK)
        inverse[into, :hi] = inverse[into, :hi] - exact(lower[i], inverse[lo:hi, :hi], 1, 0)


def inverse_kernel(place_ref, own_ref, other_ref, high_ref, low_ref, gram, inverse, held):
    for n in range(2 * FAR):
        source = own_ref if n < FAR else other_ref
        into = pl.multiple_of(place_ref[n] * SHARE, SUB)
        gram[pl.ds(into, SHARE), :] = source[(n % FAR) * SHARE : (n % FAR + 1) * SHARE, :]
    inverse[...] = jnp.zeros_like(inverse)
    row = lax.broadcasted_iota(jnp.int32, (BLOCK, BLOCK), 0)
    column = lax.broadcasted_iota(jnp.int32, (BLOCK, BLOCK), 1)

    @pl.loop(0, BLOCKS)
    def _(b):
        first = pl.multiple_of((b * (b + 1) // 2 + b) * BLOCK, BLOCK)
        held[...] = gram[pl.ds(first, BLOCK), :]
        factor_block(held)
        own = jnp.where(column <= row, held[...], 0.0)
        for step in range(BLOCKS):

            @pl.when(b == step)
            def _():
                eliminate(step, own, gram, inverse)

    high = inverse[...].astype(bf16)
    high_ref[...] = high
    low_ref[...] = (inverse[...] - high.astype(f32)).astype(bf16)


def kernel_call(kernel, place, inputs, outputs, scratch, flops):
    whole = pl.BlockSpec(memory_space=pltpu.VMEM)
    return pl.pallas_call(
        kernel,
        out_shape=outputs,
        in_specs=[pl.BlockSpec(memory_space=pltpu.SMEM)] + [whole] * len(inputs),
        out_specs=[whole] * len(outputs),
        scratch_shapes=[pltpu.VMEM(*one) for one in scratch],
        compiler_params=pltpu.CompilerParams(vmem_limit_bytes=12 << 20),
        cost_estimate=pl.CostEstimate(flops=flops, bytes_accessed=2 << 20, transcendentals=0),
    )(place, *inputs)


def inverse_factor(place, own, other):
    return kernel_call(
        inverse_kernel,
        place,
        (own, other),
        [jax.ShapeDtypeStruct((R, R), bf16)] * 2,
        [((len(PAIRS) * BLOCK, BLOCK), f32), ((R, R), f32), ((BLOCK, BLOCK), f32)],
        20 * R**3,
    )


def arrange(place, inputs, rows):
    def kernel(place_ref, *refs):
        n = 0
        for source in refs[:-1]:
            for lo in range(0, source.shape[0], rows):
                into = pl.multiple_of(place_ref[n] * rows, rows)
                refs[-1][pl.ds(into, rows), :] = source[lo : lo + rows, :]
                n += 1

    height = sum(value.shape[0] for value in inputs)
    output = jax.ShapeDtypeStruct((height, inputs[0].shape[1]), inputs[0].dtype)
    return kernel_call(kernel, place, inputs, [output], [], 1 << 20)[0]


def right_kernel(place_ref, high_ref, low_ref, *refs):
    pieces, (right_ref, own_ref, sums_ref, raw, whole) = refs[:4], refs[4:]
    quarter = R // 4
    for n in range(4):
        into = pl.multiple_of(place_ref[n] * quarter, quarter)
        raw[pl.ds(into, quarter), :] = pieces[n][...]
    for lo in range(0, R, BLOCK):
        band = slice(lo, lo + BLOCK)
        right = product(high_ref[band, :], raw[...], 1, 0) + product(low_ref[band, :], raw[...], 1, 0)
        whole[band, :] = right
        right_ref[band, :] = right.astype(bf16)
        square = right * right
        folded = added([square[:, at : at + BLOCK] for at in range(0, right.shape[1], BLOCK)])
        sums_ref[:, band] = jnp.sum(folded.T, axis=0, keepdims=True)
    rows = own_ref.shape[0]
    own_ref[...] = whole[pl.ds(pl.multiple_of(place_ref[4] * rows, rows), rows), :]


def right_side(place, high, low, pieces, rows):
    width = pieces[0].shape[1]
    return kernel_call(
        right_kernel,
        place,
        (high, low, *pieces),
        [
            jax.ShapeDtypeStruct((R, width), bf16),
            jax.ShapeDtypeStruct((rows, width), f32),
            jax.ShapeDtypeStruct((1, R), f32),
        ],
        [((R, width), bf16), ((R, width), f32)],
        4 * R * R * width,
    )


def update_kernel(place_ref, left_ref, right_ref, own_ref, inverse_ref, update_ref, factor_ref, column):
    @pl.when(pl.program_id(0) == 0)
    def _():
        rows = own_ref.shape[0]
        column[...] = jnp.broadcast_to(inverse_ref[...], (BLOCK, R)).T
        scale = column[pl.ds(pl.multiple_of(place_ref[4] * rows, rows), rows), :]
        for at in range(0, own_ref.shape[1], BLOCK):
            factor_ref[:, at : at + BLOCK] = own_ref[:, at : at + BLOCK] * scale

    scaled = (left_ref[...].astype(f32) * inverse_ref[...]).astype(bf16)
    update_ref[...] = (product(scaled, right_ref[...], 1, 0) * math.sqrt(D * FF / R)).astype(bf16)


def update_side(place, left, right, own, inverse):
    height, width = left.shape[0], right.shape[1]
    band = height // 4

    def fixed(value):
        return pl.BlockSpec(value.shape, lambda i: (0, 0))

    return pl.pallas_call(
        update_kernel,
        grid=(4,),
        out_shape=[jax.ShapeDtypeStruct((height, width), bf16), jax.ShapeDtypeStruct(own.shape, f32)],
        in_specs=[
            pl.BlockSpec(memory_space=pltpu.SMEM),
            pl.BlockSpec((band, R), lambda i: (i, 0)),
            fixed(right),
            fixed(own),
            fixed(inverse),
        ],
        out_specs=[pl.BlockSpec((band, width), lambda i: (i, 0)), fixed(own)],
        scratch_shapes=[pltpu.VMEM((R, BLOCK), f32)],
        compiler_params=pltpu.CompilerParams(vmem_limit_bytes=12 << 20),
        cost_estimate=pl.CostEstimate(flops=2 * R * height * width, bytes_accessed=4 << 20, transcendentals=0),
    )(place, left, right, own, inverse)


def from_everyone(value, axis):
    length = lax.axis_size(axis)
    return lax.all_to_all(jnp.broadcast_to(value[None], (length, *value.shape)), axis, 0, 0, tiled=True)


def from_ahead(value, axis, steps):
    length = lax.axis_size(axis)
    return lax.ppermute(value, axis, [(i, (i - steps) % length) for i in range(length)])


def ahead(value, axis):
    return [value] + [from_ahead(value, axis, steps) for steps in range(1, lax.axis_size(axis))]


def exchanged(value, axis, index):
    count = lax.axis_size(axis)
    length = value.shape[0] // count
    pieces = [lax.dynamic_slice_in_dim(value, (index + k) % count * length, length, 0) for k in range(count)]
    return [pieces[0]] + [from_ahead(pieces[count - k], axis, k) for k in range(1, count)]


def total(pieces):
    return sum((value.astype(f32) for value in pieces[1:]), pieces[0].astype(f32))


def on_device(momentum, gradient, factor):
    z_hi, y, x, z_lo, core = (lax.axis_index(name) for name in ("z_hi", "y", "x", "z_lo", "core"))
    columns = factor.shape[1]
    tensor_place = jnp.stack(
        [
            (core + c) % 2 * FAR + (x + j) % 4 * 4 + (z_lo + i) % 4
            for c in range(2)
            for j in range(4)
            for i in range(4)
        ]
    ).astype(jnp.int32)
    fsdp_place = jnp.stack([(z_hi + h) % 2 * 4 + (y + k) % 4 for h in range(2) for k in range(4)]).astype(jnp.int32)
    row_group = z_hi * 4 + y
    right_place = jnp.stack([(y + k) % 4 for k in range(4)] + [row_group]).astype(jnp.int32)

    lowered = factor.T.astype(bf16)
    near = ahead(lowered, "y")
    across = ahead(from_ahead(lowered, "z_hi", 1), "y")
    all_lowered = arrange(fsdp_place, near + across, columns)
    blended = (momentum.astype(f32) + gradient.astype(f32)).astype(bf16)
    half = blended.shape[0] // 2
    own_rows = lax.dynamic_slice_in_dim(blended, core * half, half, 0)
    other_rows = lax.dynamic_slice_in_dim(blended, (1 - core) * half, half, 0)

    sent = product(other_rows, all_lowered, 1, 1).astype(bf16)
    arrived = from_ahead(sent, "core", 1)
    partial_left = (product(own_rows, all_lowered, 1, 1) + arrived.astype(f32)).astype(bf16)
    left_line = total(exchanged(partial_left, "x", x)).astype(bf16)
    left_rows = total(exchanged(left_line, "z_lo", z_lo)).astype(bf16)
    left_line = jnp.concatenate(ahead(left_rows, "z_lo"))
    own_left = jnp.concatenate(ahead(left_line, "x"))
    other_left = from_ahead(own_left, "core", 1)

    local_gram = product(own_left, own_left, 0, 0) + product(other_left, other_left, 0, 0)
    packed = jnp.concatenate(
        [local_gram[i * BLOCK : (i + 1) * BLOCK, j * BLOCK : (j + 1) * BLOCK] for i, j in PAIRS]
    )
    piece = lax.dynamic_slice_in_dim(packed, (core * FAR + x * 4 + z_lo) * SHARE, SHARE, 0)
    summed = jnp.sum(from_everyone(piece, ("z_hi", "y")), axis=0)

    left_factor = arrange(tensor_place, (own_left, other_left), half // FAR)
    partial_right = product(left_factor, blended, 0, 0).astype(bf16)
    received = exchanged(partial_right, "y", y)

    gram_line = jnp.concatenate(ahead(summed, "z_lo"))
    gram_line, *received = lax.optimization_barrier((gram_line, *received))
    right_rows = total(received).astype(bf16)
    gram_line, right_rows = lax.optimization_barrier((gram_line, right_rows))
    opposite = from_ahead(right_rows, "z_hi", 1)
    opposite, *gram_lines = lax.optimization_barrier((opposite, *ahead(gram_line, "x")))
    own_gram = jnp.concatenate(gram_lines)
    other_gram = from_ahead(own_gram, "core", 1)
    right_rows = total([right_rows, opposite]).astype(bf16)
    other_gram, right_rows = lax.optimization_barrier((other_gram, right_rows))
    right_pieces = ahead(right_rows, "y")
    high, low = inverse_factor(tensor_place, own_gram, other_gram)
    right_factor, own_right, own_sums = right_side(right_place, high, low, right_pieces, columns)

    last_left, own_sums = lax.optimization_barrier((left_factor, own_sums))
    square_sums = jnp.sum(from_everyone(own_sums, TENSOR), axis=(0, 1))
    orthonormal = (product(last_left, high, 1, 1) + product(last_left, low, 1, 1)).astype(bf16)
    taken = product(orthonormal, right_factor, 1, 0)
    new_momentum = (blended.astype(f32) - (1.0 - decay_rate) * taken).astype(bf16)
    inverse = lax.rsqrt(square_sums + epsilon)[None]
    update, own_factor = update_side(right_place, orthonormal, right_factor, own_right, inverse)
    return (new_momentum, own_factor.T, update)


def solution(mesh):
    torus = Mesh(mesh.devices.reshape(2, 4, 4, 4, 2), ("z_hi", "y", "x", "z_lo", "core"))
    fsdp = ("z_hi", "y")
    return jax.shard_map(
        on_device,
        mesh=torus,
        in_specs=(P(fsdp, TENSOR), P(fsdp, TENSOR), P(TENSOR, fsdp)),
        out_specs=(P(fsdp, TENSOR), P(TENSOR, fsdp), P(fsdp, TENSOR)),
        check_vma=False,
    )
```

```python
import math

import jax
import jax.numpy as jnp
from jax import lax
from jax.experimental import pallas as pl
from jax.experimental.pallas import tpu as pltpu
from jax.sharding import Mesh
from jax.sharding import PartitionSpec as P

D = 8192
FF = 28672
R = 512
FAR = 16
BLOCK = 128
BLOCKS = R // BLOCK
PAIRS = [(i, j) for i in range(BLOCKS) for j in range(i + 1)]
SHARE = len(PAIRS) * BLOCK // (2 * FAR)
SUB = 8
TENSOR = ("x", "z_lo", "core")

decay_rate = 0.95
epsilon = 1e-06
f32 = jnp.float32
bf16 = jnp.bfloat16


def product(left, right, left_dim, right_dim):
    return lax.dot_general(left, right, (((left_dim,), (right_dim,)), ((), ())), preferred_element_type=f32)


def added(terms):
    while len(terms) > 1:
        terms = [
            terms[i] + terms[i + 1] if i + 1 < len(terms) else terms[i] for i in range(0, len(terms), 2)
        ]
    return terms[0]


def spread(value):
    return jnp.broadcast_to(value, (SUB, BLOCK))


def small_inverse(entries):
    rest = [row[:] for row in entries]
    inverse = [None] * SUB
    upper = [[None] * SUB for _ in range(SUB)]
    for j in range(SUB):
        inverse[j] = lax.rsqrt(rest[j][j])
        for k in range(j + 1, SUB):
            upper[j][k] = rest[j][k] * inverse[j]
        for i in range(j + 1, SUB):
            for k in range(i, SUB):
                rest[i][k] = rest[i][k] - upper[j][i] * upper[j][k]
    result = [[None] * SUB for _ in range(SUB)]
    for j in range(SUB):
        result[j][j] = inverse[j]
        for i in range(j + 1, SUB):
            total = upper[j][i] * result[j][j]
            for k in range(j + 1, i):
                total = total + upper[k][i] * result[k][j]
            result[i][j] = -(inverse[i] * total)
    return result


def in_three(value):
    first = value.astype(bf16)
    rest = value - first.astype(f32)
    second = rest.astype(bf16)
    return first, second, (rest - second.astype(f32)).astype(bf16)


def exact(left, right, left_dim, right_dim):
    a, b, c = in_three(left)
    d, e, f = in_three(right)
    lefts = jnp.concatenate([a, a, b, b, a, c], axis=left_dim)
    rights = jnp.concatenate([d, e, d, e, f, d], axis=right_dim)
    return product(lefts, rights, left_dim, right_dim)


def factor_block(held):
    sub = lax.broadcasted_iota(jnp.int32, (SUB, BLOCK), 0)
    lane = lax.broadcasted_iota(jnp.int32, (SUB, BLOCK), 1)
    lane_row = lax.broadcasted_iota(jnp.int32, (1, BLOCK), 1)
    rows, following = held[:SUB, :], held[SUB : 2 * SUB, :]
    for lo in range(0, BLOCK, SUB):
        inside = (lane >= lo) & (lane < lo + SUB)
        lanes = [spread(rows[:, lo + k : lo + k + 1]) for k in range(SUB)]
        entries = [[spread(lanes[k][i : i + 1, :]) if k >= i else None for k in range(SUB)] for i in range(SUB)]
        inverse = small_inverse(entries)
        bare = [
            jnp.where(lane == lo + k, 1.0, jnp.where(inside, 0.0, spread(rows[k : k + 1, :]))) for k in range(SUB)
        ]
        done = [added([inverse[i][k] * bare[k] for k in range(i + 1)]) for i in range(SUB)]
        packed = done[0]
        for i in range(1, SUB):
            packed = jnp.where(sub == i, done[i], packed)
        held[lo : lo + SUB, :] = packed
        if lo + SUB < BLOCK:
            weights = [added([inverse[m][k] * done[m] for m in range(k, SUB)]) for k in range(SUB)]

            def brought(later):
                terms = [spread(later[:, lo + k : lo + k + 1]) * weights[k] for k in range(SUB)]
                return jnp.where(inside, 0.0, later) - added(terms)

            rows = brought(following)
        if lo + 2 * SUB < BLOCK:
            following = brought(held[lo + 2 * SUB : lo + 3 * SUB, :])
        if lo + 3 * SUB < BLOCK:
            change = exact(packed, packed, 0, 0)
            kept = jnp.where((lane_row >= lo) & (lane_row < lo + SUB), 0.0, held[lo + 3 * SUB :, :])
            held[lo + 3 * SUB :, :] = kept - change[lo + 3 * SUB :, :]


FIRST = {pair: n * BLOCK for n, pair in enumerate(PAIRS)}


def eliminate(b, own, gram, inverse):
    def block(i, j):
        return gram[FIRST[i, j] : FIRST[i, j] + BLOCK, :]

    lo, hi = b * BLOCK, (b + 1) * BLOCK
    if b:
        inverse[lo:hi, :lo] = exact(own, inverse[lo:hi, :lo], 1, 0)
    inverse[lo:hi, lo:hi] = own
    lower = {i: exact(block(i, b), own, 1, 1) for i in range(b + 1, BLOCKS)}
    for i in range(b + 1, BLOCKS):
        for j in range(b + 1, i + 1):
            gram[FIRST[i, j] : FIRST[i, j] + BLOCK, :] = block(i, j) - exact(lower[i], lower[j], 1, 1)
        into = slice(i * BLOCK, (i + 1) * BLOCK)
        inverse[into, :hi] = inverse[into, :hi] - exact(lower[i], inverse[lo:hi, :hi], 1, 0)


def inverse_kernel(place_ref, own_ref, other_ref, high_ref, low_ref, gram, inverse, held):
    for n in range(2 * FAR):
        source = own_ref if n < FAR else other_ref
        into = pl.multiple_of(place_ref[n] * SHARE, SUB)
        gram[pl.ds(into, SHARE), :] = source[(n % FAR) * SHARE : (n % FAR + 1) * SHARE, :]
    inverse[...] = jnp.zeros_like(inverse)
    row = lax.broadcasted_iota(jnp.int32, (BLOCK, BLOCK), 0)
    column = lax.broadcasted_iota(jnp.int32, (BLOCK, BLOCK), 1)

    @pl.loop(0, BLOCKS)
    def _(b):
        first = pl.multiple_of((b * (b + 1) // 2 + b) * BLOCK, BLOCK)
        held[...] = gram[pl.ds(first, BLOCK), :]
        factor_block(held)
        own = jnp.where(column <= row, held[...], 0.0)
        for step in range(BLOCKS):

            @pl.when(b == step)
            def _():
                eliminate(step, own, gram, inverse)

    high = inverse[...].astype(bf16)
    high_ref[...] = high
    low_ref[...] = (inverse[...] - high.astype(f32)).astype(bf16)


def kernel_call(kernel, place, inputs, outputs, scratch, flops):
    whole = pl.BlockSpec(memory_space=pltpu.VMEM)
    return pl.pallas_call(
        kernel,
        out_shape=outputs,
        in_specs=[pl.BlockSpec(memory_space=pltpu.SMEM)] + [whole] * len(inputs),
        out_specs=[whole] * len(outputs),
        scratch_shapes=[pltpu.VMEM(*one) for one in scratch],
        compiler_params=pltpu.CompilerParams(vmem_limit_bytes=12 << 20),
        cost_estimate=pl.CostEstimate(flops=flops, bytes_accessed=2 << 20, transcendentals=0),
    )(place, *inputs)


def inverse_factor(place, own, other):
    return kernel_call(
        inverse_kernel,
        place,
        (own, other),
        [jax.ShapeDtypeStruct((R, R), bf16)] * 2,
        [((len(PAIRS) * BLOCK, BLOCK), f32), ((R, R), f32), ((BLOCK, BLOCK), f32)],
        20 * R**3,
    )


def arrange(place, inputs, rows):
    def kernel(place_ref, *refs):
        n = 0
        for source in refs[:-1]:
            for lo in range(0, source.shape[0], rows):
                into = pl.multiple_of(place_ref[n] * rows, rows)
                refs[-1][pl.ds(into, rows), :] = source[lo : lo + rows, :]
                n += 1

    height = sum(value.shape[0] for value in inputs)
    output = jax.ShapeDtypeStruct((height, inputs[0].shape[1]), inputs[0].dtype)
    return kernel_call(kernel, place, inputs, [output], [], 1 << 20)[0]


def right_kernel(place_ref, high_ref, low_ref, *refs):
    pieces, (right_ref, own_ref, sums_ref, raw, whole) = refs[:4], refs[4:]
    quarter = R // 4
    for n in range(4):
        into = pl.multiple_of(place_ref[n] * quarter, quarter)
        raw[pl.ds(into, quarter), :] = pieces[n][...]
    for lo in range(0, R, BLOCK):
        band = slice(lo, lo + BLOCK)
        right = product(high_ref[band, :], raw[...], 1, 0) + product(low_ref[band, :], raw[...], 1, 0)
        whole[band, :] = right
        right_ref[band, :] = right.astype(bf16)
        square = right * right
        folded = added([square[:, at : at + BLOCK] for at in range(0, right.shape[1], BLOCK)])
        sums_ref[:, band] = jnp.sum(folded.T, axis=0, keepdims=True)
    rows = own_ref.shape[0]
    own_ref[...] = whole[pl.ds(pl.multiple_of(place_ref[4] * rows, rows), rows), :]


def right_side(place, high, low, pieces, rows):
    width = pieces[0].shape[1]
    return kernel_call(
        right_kernel,
        place,
        (high, low, *pieces),
        [
            jax.ShapeDtypeStruct((R, width), bf16),
            jax.ShapeDtypeStruct((rows, width), f32),
            jax.ShapeDtypeStruct((1, R), f32),
        ],
        [((R, width), bf16), ((R, width), f32)],
        4 * R * R * width,
    )


def update_kernel(place_ref, left_ref, right_ref, own_ref, inverse_ref, update_ref, factor_ref, column):
    @pl.when(pl.program_id(0) == 0)
    def _():
        rows = own_ref.shape[0]
        column[...] = jnp.broadcast_to(inverse_ref[...], (BLOCK, R)).T
        scale = column[pl.ds(pl.multiple_of(place_ref[4] * rows, rows), rows), :]
        for at in range(0, own_ref.shape[1], BLOCK):
            factor_ref[:, at : at + BLOCK] = own_ref[:, at : at + BLOCK] * scale

    scaled = (left_ref[...].astype(f32) * inverse_ref[...]).astype(bf16)
    update_ref[...] = (product(scaled, right_ref[...], 1, 0) * math.sqrt(D * FF / R)).astype(bf16)


def update_side(place, left, right, own, inverse):
    height, width = left.shape[0], right.shape[1]
    band = height // 4

    def fixed(value):
        return pl.BlockSpec(value.shape, lambda i: (0, 0))

    return pl.pallas_call(
        update_kernel,
        grid=(4,),
        out_shape=[jax.ShapeDtypeStruct((height, width), bf16), jax.ShapeDtypeStruct(own.shape, f32)],
        in_specs=[
            pl.BlockSpec(memory_space=pltpu.SMEM),
            pl.BlockSpec((band, R), lambda i: (i, 0)),
            fixed(right),
            fixed(own),
            fixed(inverse),
        ],
        out_specs=[pl.BlockSpec((band, width), lambda i: (i, 0)), fixed(own)],
        scratch_shapes=[pltpu.VMEM((R, BLOCK), f32)],
        compiler_params=pltpu.CompilerParams(vmem_limit_bytes=12 << 20),
        cost_estimate=pl.CostEstimate(flops=2 * R * height * width, bytes_accessed=4 << 20, transcendentals=0),
    )(place, left, right, own, inverse)


def from_everyone(value, axis):
    length = lax.axis_size(axis)
    return lax.all_to_all(jnp.broadcast_to(value[None], (length, *value.shape)), axis, 0, 0, tiled=True)


def from_ahead(value, axis, steps):
    length = lax.axis_size(axis)
    return lax.ppermute(value, axis, [(i, (i - steps) % length) for i in range(length)])


def ahead(value, axis):
    return [value] + [from_ahead(value, axis, steps) for steps in range(1, lax.axis_size(axis))]


def exchanged(value, axis, index):
    count = lax.axis_size(axis)
    length = value.shape[0] // count
    pieces = [lax.dynamic_slice_in_dim(value, (index + k) % count * length, length, 0) for k in range(count)]
    return [pieces[0]] + [from_ahead(pieces[count - k], axis, k) for k in range(1, count)]


def total(pieces):
    return sum((value.astype(f32) for value in pieces[1:]), pieces[0].astype(f32))


def on_device(momentum, gradient, factor):
    z_hi, y, x, z_lo, core = (lax.axis_index(name) for name in ("z_hi", "y", "x", "z_lo", "core"))
    columns = factor.shape[1]
    gram_place = jnp.stack(
        [(core + c) % 2 * FAR + (x + j) % 4 * 4 + i for c in range(2) for j in range(4) for i in range(4)]
    ).astype(jnp.int32)
    core_place = jnp.stack([core, 1 - core]).astype(jnp.int32)
    fsdp_place = jnp.stack([(z_hi + h) % 2 * 4 + (y + k) % 4 for h in range(2) for k in range(4)]).astype(jnp.int32)
    row_group = z_hi * 4 + y
    right_place = jnp.stack([(y + k) % 4 for k in range(4)] + [row_group]).astype(jnp.int32)

    lowered = factor.T.astype(bf16)
    near = ahead(lowered, "y")
    across = ahead(from_ahead(lowered, "z_hi", 1), "y")
    all_lowered = arrange(fsdp_place, near + across, columns)
    blended = (momentum.astype(f32) + gradient.astype(f32)).astype(bf16)
    half = blended.shape[0] // 2
    own_rows = lax.dynamic_slice_in_dim(blended, core * half, half, 0)
    other_rows = lax.dynamic_slice_in_dim(blended, (1 - core) * half, half, 0)

    sent = product(other_rows, all_lowered, 1, 1).astype(bf16)
    arrived = from_ahead(sent, "core", 1)
    partial_left = (product(own_rows, all_lowered, 1, 1) + arrived.astype(f32)).astype(bf16)
    left_line = total(exchanged(partial_left, "x", x)).astype(bf16)
    left_rows = total(exchanged(left_line, "z_lo", z_lo)).astype(bf16)
    own_left = from_everyone(left_rows, ("x", "z_lo")).reshape(half, R)
    other_left = from_ahead(own_left, "core", 1)

    local_gram = product(own_left, own_left, 0, 0) + product(other_left, other_left, 0, 0)
    packed = jnp.concatenate(
        [local_gram[i * BLOCK : (i + 1) * BLOCK, j * BLOCK : (j + 1) * BLOCK] for i, j in PAIRS]
    )
    piece = lax.dynamic_slice_in_dim(packed, (core * FAR + x * 4 + z_lo) * SHARE, SHARE, 0)
    summed = jnp.sum(from_everyone(piece, ("z_hi", "y")), axis=0)

    left_factor = arrange(core_place, (own_left, other_left), half)
    partial_right = product(left_factor, blended, 0, 0).astype(bf16)
    received = exchanged(partial_right, "y", y)

    gram_line = from_everyone(summed, "z_lo").reshape(4 * SHARE, BLOCK)
    gram_line, *received = lax.optimization_barrier((gram_line, *received))
    right_rows = total(received).astype(bf16)
    gram_line, right_rows = lax.optimization_barrier((gram_line, right_rows))
    opposite = from_ahead(right_rows, "z_hi", 1)
    opposite, *gram_lines = lax.optimization_barrier((opposite, *ahead(gram_line, "x")))
    own_gram = jnp.concatenate(gram_lines)
    other_gram = from_ahead(own_gram, "core", 1)
    right_rows = total([right_rows, opposite]).astype(bf16)
    other_gram, right_rows = lax.optimization_barrier((other_gram, right_rows))
    right_pieces = ahead(right_rows, "y")
    high, low = inverse_factor(gram_place, own_gram, other_gram)
    right_factor, own_right, own_sums = right_side(right_place, high, low, right_pieces, columns)

    last_left, own_sums = lax.optimization_barrier((left_factor, own_sums))
    square_sums = jnp.sum(from_everyone(own_sums, TENSOR), axis=(0, 1))
    orthonormal = (product(last_left, high, 1, 1) + product(last_left, low, 1, 1)).astype(bf16)
    taken = product(orthonormal, right_factor, 1, 0)
    new_momentum = (blended.astype(f32) - (1.0 - decay_rate) * taken).astype(bf16)
    inverse = lax.rsqrt(square_sums + epsilon)[None]
    update, own_factor = update_side(right_place, orthonormal, right_factor, own_right, inverse)
    return (new_momentum, own_factor.T, update)


def solution(mesh):
    torus = Mesh(mesh.devices.reshape(2, 4, 4, 4, 2), ("z_hi", "y", "x", "z_lo", "core"))
    fsdp = ("z_hi", "y")
    return jax.shard_map(
        on_device,
        mesh=torus,
        in_specs=(P(fsdp, TENSOR), P(fsdp, TENSOR), P(TENSOR, fsdp)),
        out_specs=(P(fsdp, TENSOR), P(TENSOR, fsdp), P(fsdp, TENSOR)),
        check_vma=False,
    )
```

```python
import math

import jax
import jax.numpy as jnp
from jax import lax
from jax.experimental import pallas as pl
from jax.experimental.pallas import tpu as pltpu
from jax.sharding import Mesh
from jax.sharding import PartitionSpec as P

D = 8192
FF = 28672
R = 512
FAR = 16
BLOCK = 128
BLOCKS = R // BLOCK
PAIRS = [(i, j) for i in range(BLOCKS) for j in range(i + 1)]
SHARE = len(PAIRS) * BLOCK // (2 * FAR)
SUB = 8
TENSOR = ("x", "z_lo", "core")

decay_rate = 0.95
epsilon = 1e-06
f32 = jnp.float32
bf16 = jnp.bfloat16


def product(left, right, left_dim, right_dim):
    return lax.dot_general(left, right, (((left_dim,), (right_dim,)), ((), ())), preferred_element_type=f32)


def added(terms):
    while len(terms) > 1:
        terms = [
            terms[i] + terms[i + 1] if i + 1 < len(terms) else terms[i] for i in range(0, len(terms), 2)
        ]
    return terms[0]


def spread(value):
    return jnp.broadcast_to(value, (SUB, BLOCK))


def small_inverse(entries):
    rest = [row[:] for row in entries]
    inverse = [None] * SUB
    upper = [[None] * SUB for _ in range(SUB)]
    for j in range(SUB):
        inverse[j] = lax.rsqrt(rest[j][j])
        for k in range(j + 1, SUB):
            upper[j][k] = rest[j][k] * inverse[j]
        for i in range(j + 1, SUB):
            for k in range(i, SUB):
                rest[i][k] = rest[i][k] - upper[j][i] * upper[j][k]
    result = [[None] * SUB for _ in range(SUB)]
    for j in range(SUB):
        result[j][j] = inverse[j]
        for i in range(j + 1, SUB):
            total = upper[j][i] * result[j][j]
            for k in range(j + 1, i):
                total = total + upper[k][i] * result[k][j]
            result[i][j] = -(inverse[i] * total)
    return result


def in_three(value):
    first = value.astype(bf16)
    rest = value - first.astype(f32)
    second = rest.astype(bf16)
    return first, second, (rest - second.astype(f32)).astype(bf16)


def exact(left, right, left_dim, right_dim):
    a, b, c = in_three(left)
    d, e, f = in_three(right)
    lefts = jnp.concatenate([a, a, b, b, a, c], axis=left_dim)
    rights = jnp.concatenate([d, e, d, e, f, d], axis=right_dim)
    return product(lefts, rights, left_dim, right_dim)


def factor_block(held):
    sub = lax.broadcasted_iota(jnp.int32, (SUB, BLOCK), 0)
    lane = lax.broadcasted_iota(jnp.int32, (SUB, BLOCK), 1)
    lane_row = lax.broadcasted_iota(jnp.int32, (1, BLOCK), 1)
    rows, following = held[:SUB, :], held[SUB : 2 * SUB, :]
    for lo in range(0, BLOCK, SUB):
        inside = (lane >= lo) & (lane < lo + SUB)
        lanes = [spread(rows[:, lo + k : lo + k + 1]) for k in range(SUB)]
        entries = [[spread(lanes[k][i : i + 1, :]) if k >= i else None for k in range(SUB)] for i in range(SUB)]
        inverse = small_inverse(entries)
        bare = [
            jnp.where(lane == lo + k, 1.0, jnp.where(inside, 0.0, spread(rows[k : k + 1, :]))) for k in range(SUB)
        ]
        done = [added([inverse[i][k] * bare[k] for k in range(i + 1)]) for i in range(SUB)]
        packed = done[0]
        for i in range(1, SUB):
            packed = jnp.where(sub == i, done[i], packed)
        held[lo : lo + SUB, :] = packed
        if lo + SUB < BLOCK:
            weights = [added([inverse[m][k] * done[m] for m in range(k, SUB)]) for k in range(SUB)]

            def brought(later):
                terms = [spread(later[:, lo + k : lo + k + 1]) * weights[k] for k in range(SUB)]
                return jnp.where(inside, 0.0, later) - added(terms)

            rows = brought(following)
        if lo + 2 * SUB < BLOCK:
            following = brought(held[lo + 2 * SUB : lo + 3 * SUB, :])
        if lo + 3 * SUB < BLOCK:
            change = exact(packed, packed, 0, 0)
            kept = jnp.where((lane_row >= lo) & (lane_row < lo + SUB), 0.0, held[lo + 3 * SUB :, :])
            held[lo + 3 * SUB :, :] = kept - change[lo + 3 * SUB :, :]


FIRST = {pair: n * BLOCK for n, pair in enumerate(PAIRS)}


def eliminate(b, own, gram, inverse):
    def block(i, j):
        return gram[FIRST[i, j] : FIRST[i, j] + BLOCK, :]

    lo, hi = b * BLOCK, (b + 1) * BLOCK
    if b:
        inverse[lo:hi, :lo] = exact(own, inverse[lo:hi, :lo], 1, 0)
    inverse[lo:hi, lo:hi] = own
    lower = {i: exact(block(i, b), own, 1, 1) for i in range(b + 1, BLOCKS)}
    for i in range(b + 1, BLOCKS):
        for j in range(b + 1, i + 1):
            gram[FIRST[i, j] : FIRST[i, j] + BLOCK, :] = block(i, j) - exact(lower[i], lower[j], 1, 1)
        into = slice(i * BLOCK, (i + 1) * BLOCK)
        inverse[into, :hi] = inverse[into, :hi] - exact(lower[i], inverse[lo:hi, :hi], 1, 0)


def inverse_kernel(place_ref, own_ref, other_ref, high_ref, low_ref, gram, inverse, held):
    for n in range(2 * FAR):
        source = own_ref if n < FAR else other_ref
        into = pl.multiple_of(place_ref[n] * SHARE, SUB)
        gram[pl.ds(into, SHARE), :] = source[(n % FAR) * SHARE : (n % FAR + 1) * SHARE, :]
    inverse[...] = jnp.zeros_like(inverse)
    row = lax.broadcasted_iota(jnp.int32, (BLOCK, BLOCK), 0)
    column = lax.broadcasted_iota(jnp.int32, (BLOCK, BLOCK), 1)

    @pl.loop(0, BLOCKS)
    def _(b):
        first = pl.multiple_of((b * (b + 1) // 2 + b) * BLOCK, BLOCK)
        held[...] = gram[pl.ds(first, BLOCK), :]
        factor_block(held)
        own = jnp.where(column <= row, held[...], 0.0)
        for step in range(BLOCKS):

            @pl.when(b == step)
            def _():
                eliminate(step, own, gram, inverse)

    high = inverse[...].astype(bf16)
    high_ref[...] = high
    low_ref[...] = (inverse[...] - high.astype(f32)).astype(bf16)


def kernel_call(kernel, place, inputs, outputs, scratch, flops):
    whole = pl.BlockSpec(memory_space=pltpu.VMEM)
    return pl.pallas_call(
        kernel,
        out_shape=outputs,
        in_specs=[pl.BlockSpec(memory_space=pltpu.SMEM)] + [whole] * len(inputs),
        out_specs=[whole] * len(outputs),
        scratch_shapes=[pltpu.VMEM(*one) for one in scratch],
        compiler_params=pltpu.CompilerParams(vmem_limit_bytes=12 << 20),
        cost_estimate=pl.CostEstimate(flops=flops, bytes_accessed=2 << 20, transcendentals=0),
    )(place, *inputs)


def inverse_factor(place, own, other):
    return kernel_call(
        inverse_kernel,
        place,
        (own, other),
        [jax.ShapeDtypeStruct((R, R), bf16)] * 2,
        [((len(PAIRS) * BLOCK, BLOCK), f32), ((R, R), f32), ((BLOCK, BLOCK), f32)],
        20 * R**3,
    )


def arrange(place, inputs, rows):
    def kernel(place_ref, *refs):
        n = 0
        for source in refs[:-1]:
            for lo in range(0, source.shape[0], rows):
                into = pl.multiple_of(place_ref[n] * rows, rows)
                refs[-1][pl.ds(into, rows), :] = source[lo : lo + rows, :]
                n += 1

    height = sum(value.shape[0] for value in inputs)
    output = jax.ShapeDtypeStruct((height, inputs[0].shape[1]), inputs[0].dtype)
    return kernel_call(kernel, place, inputs, [output], [], 1 << 20)[0]


def right_kernel(place_ref, high_ref, low_ref, *refs):
    pieces, (right_ref, own_ref, sums_ref, raw, whole) = refs[:4], refs[4:]
    quarter = R // 4
    for n in range(4):
        into = pl.multiple_of(place_ref[n] * quarter, quarter)
        raw[pl.ds(into, quarter), :] = pieces[n][...]
    for lo in range(0, R, BLOCK):
        band = slice(lo, lo + BLOCK)
        right = product(high_ref[band, :], raw[...], 1, 0) + product(low_ref[band, :], raw[...], 1, 0)
        whole[band, :] = right
        right_ref[band, :] = right.astype(bf16)
        square = right * right
        folded = added([square[:, at : at + BLOCK] for at in range(0, right.shape[1], BLOCK)])
        row = jnp.sum(folded.T, axis=0, keepdims=True)
        sums_ref[:, :, band] = jnp.broadcast_to(row[None], (2 * FAR, 1, BLOCK))
    rows = own_ref.shape[0]
    own_ref[...] = whole[pl.ds(pl.multiple_of(place_ref[4] * rows, rows), rows), :]


def right_side(place, high, low, pieces, rows):
    width = pieces[0].shape[1]
    return kernel_call(
        right_kernel,
        place,
        (high, low, *pieces),
        [
            jax.ShapeDtypeStruct((R, width), bf16),
            jax.ShapeDtypeStruct((rows, width), f32),
            jax.ShapeDtypeStruct((2 * FAR, 1, R), f32),
        ],
        [((R, width), bf16), ((R, width), f32)],
        4 * R * R * width,
    )


def update_kernel(place_ref, left_ref, right_ref, own_ref, sums_ref, update_ref, factor_ref, inverse, column):
    step = pl.program_id(0)

    @pl.when(step == 0)
    def _():
        inverse[...] = lax.rsqrt(jnp.sum(sums_ref[...], axis=0) + epsilon)
        column[...] = jnp.broadcast_to(inverse[...], (BLOCK, R)).T
        rows = own_ref.shape[0]
        scale = column[pl.ds(pl.multiple_of(place_ref[4] * rows, rows), rows), :]
        for at in range(0, own_ref.shape[1], BLOCK):
            factor_ref[:, at : at + BLOCK] = own_ref[:, at : at + BLOCK] * scale

    band = update_ref.shape[0]
    left = left_ref[pl.ds(pl.multiple_of(step * band, band), band), :]
    scaled = (left.astype(f32) * inverse[...]).astype(bf16)
    update_ref[...] = (product(scaled, right_ref[...], 1, 0) * math.sqrt(D * FF / R)).astype(bf16)


def update_side(place, left, right, own, sums):
    height, width = left.shape[0], right.shape[1]
    steps = 4
    whole = pl.BlockSpec(memory_space=pltpu.VMEM)
    return pl.pallas_call(
        update_kernel,
        grid=(steps,),
        out_shape=[jax.ShapeDtypeStruct((height, width), bf16), jax.ShapeDtypeStruct(own.shape, f32)],
        in_specs=[pl.BlockSpec(memory_space=pltpu.SMEM)] + [whole] * 4,
        out_specs=[
            pl.BlockSpec((height // steps, width), lambda i: (i, 0)),
            pl.BlockSpec(own.shape, lambda i: (0, 0)),
        ],
        scratch_shapes=[pltpu.VMEM((1, R), f32), pltpu.VMEM((R, BLOCK), f32)],
        compiler_params=pltpu.CompilerParams(vmem_limit_bytes=12 << 20),
        cost_estimate=pl.CostEstimate(flops=2 * R * height * width, bytes_accessed=4 << 20, transcendentals=0),
    )(place, left, right, own, sums)


def from_everyone(value, axis):
    length = lax.axis_size(axis)
    return lax.all_to_all(jnp.broadcast_to(value[None], (length, *value.shape)), axis, 0, 0, tiled=True)


def from_ahead(value, axis, steps):
    length = lax.axis_size(axis)
    return lax.ppermute(value, axis, [(i, (i - steps) % length) for i in range(length)])


def ahead(value, axis):
    return [value] + [from_ahead(value, axis, steps) for steps in range(1, lax.axis_size(axis))]


def exchanged(value, axis, index):
    count = lax.axis_size(axis)
    length = value.shape[0] // count
    pieces = [lax.dynamic_slice_in_dim(value, (index + k) % count * length, length, 0) for k in range(count)]
    return [pieces[0]] + [from_ahead(pieces[count - k], axis, k) for k in range(1, count)]


def total(pieces):
    return sum((value.astype(f32) for value in pieces[1:]), pieces[0].astype(f32))


def on_device(momentum, gradient, factor):
    z_hi, y, x, z_lo, core = (lax.axis_index(name) for name in ("z_hi", "y", "x", "z_lo", "core"))
    columns = factor.shape[1]
    gram_place = jnp.stack(
        [(core + c) % 2 * FAR + (x + j) % 4 * 4 + i for c in range(2) for j in range(4) for i in range(4)]
    ).astype(jnp.int32)
    core_place = jnp.stack([core, 1 - core]).astype(jnp.int32)
    fsdp_place = jnp.stack([(z_hi + h) % 2 * 4 + (y + k) % 4 for h in range(2) for k in range(4)]).astype(jnp.int32)
    row_group = z_hi * 4 + y
    right_place = jnp.stack([(y + k) % 4 for k in range(4)] + [row_group]).astype(jnp.int32)

    lowered = factor.T.astype(bf16)
    near = ahead(lowered, "y")
    across = ahead(from_ahead(lowered, "z_hi", 1), "y")
    all_lowered = arrange(fsdp_place, near + across, columns)
    blended = (momentum.astype(f32) + gradient.astype(f32)).astype(bf16)
    half = blended.shape[0] // 2
    own_rows = lax.dynamic_slice_in_dim(blended, core * half, half, 0)
    other_rows = lax.dynamic_slice_in_dim(blended, (1 - core) * half, half, 0)

    sent = product(other_rows, all_lowered, 1, 1).astype(bf16)
    arrived = from_ahead(sent, "core", 1)
    kept = lax.optimization_barrier(product(own_rows, all_lowered, 1, 1))
    partial_left = (kept + arrived.astype(f32)).astype(bf16)
    left_line = total(exchanged(partial_left, "x", x)).astype(bf16)
    left_rows = total(exchanged(left_line, "z_lo", z_lo)).astype(bf16)
    own_left = from_everyone(left_rows, ("x", "z_lo")).reshape(half, R)
    other_left = from_ahead(own_left, "core", 1)

    local_gram = product(own_left, own_left, 0, 0) + product(other_left, other_left, 0, 0)
    packed = jnp.concatenate(
        [local_gram[i * BLOCK : (i + 1) * BLOCK, j * BLOCK : (j + 1) * BLOCK] for i, j in PAIRS]
    )
    piece = lax.dynamic_slice_in_dim(packed, (core * FAR + x * 4 + z_lo) * SHARE, SHARE, 0)
    summed = jnp.sum(from_everyone(piece, ("z_hi", "y")), axis=0)

    left_factor = arrange(core_place, (own_left, other_left), half)
    partial_right = product(left_factor, blended, 0, 0).astype(bf16)
    received = exchanged(partial_right, "y", y)

    gram_line = from_everyone(summed, "z_lo").reshape(4 * SHARE, BLOCK)
    gram_line, *received = lax.optimization_barrier((gram_line, *received))
    right_rows = total(received).astype(bf16)
    gram_line, right_rows = lax.optimization_barrier((gram_line, right_rows))
    opposite = from_ahead(right_rows, "z_hi", 1)
    opposite, *gram_lines = lax.optimization_barrier((opposite, *ahead(gram_line, "x")))
    own_gram = jnp.concatenate(gram_lines)
    other_gram = from_ahead(own_gram, "core", 1)
    right_rows = total([right_rows, opposite]).astype(bf16)
    other_gram, right_rows = lax.optimization_barrier((other_gram, right_rows))
    right_pieces = ahead(right_rows, "y")
    high, low = inverse_factor(gram_place, own_gram, other_gram)
    right_factor, own_right, own_sums = right_side(right_place, high, low, right_pieces, columns)

    last_left = left_factor
    sums = lax.all_to_all(own_sums, TENSOR, 0, 0, tiled=True)
    orthonormal = (product(last_left, high, 1, 1) + product(last_left, low, 1, 1)).astype(bf16)
    taken = product(orthonormal, right_factor, 1, 0)
    new_momentum = (blended.astype(f32) - (1.0 - decay_rate) * taken).astype(bf16)
    update, own_factor = update_side(right_place, orthonormal, right_factor, own_right, sums)
    return (new_momentum, own_factor.T, update)


def solution(mesh):
    torus = Mesh(mesh.devices.reshape(2, 4, 4, 4, 2), ("z_hi", "y", "x", "z_lo", "core"))
    fsdp = ("z_hi", "y")
    return jax.shard_map(
        on_device,
        mesh=torus,
        in_specs=(P(fsdp, TENSOR), P(fsdp, TENSOR), P(TENSOR, fsdp)),
        out_specs=(P(fsdp, TENSOR), P(TENSOR, fsdp), P(fsdp, TENSOR)),
        check_vma=False,
    )
```

```python
import math

import jax
import jax.numpy as jnp
from jax import lax
from jax.experimental import pallas as pl
from jax.experimental.pallas import tpu as pltpu
from jax.sharding import Mesh
from jax.sharding import PartitionSpec as P

D = 8192
FF = 28672
R = 512
FAR = 16
BLOCK = 128
BLOCKS = R // BLOCK
PAIRS = [(i, j) for i in range(BLOCKS) for j in range(i + 1)]
SHARE = len(PAIRS) * BLOCK // (2 * FAR)
SUB = 8
TENSOR = ("x", "z_lo", "core")

decay_rate = 0.95
epsilon = 1e-06
f32 = jnp.float32
bf16 = jnp.bfloat16


def product(left, right, left_dim, right_dim):
    return lax.dot_general(left, right, (((left_dim,), (right_dim,)), ((), ())), preferred_element_type=f32)


def added(terms):
    while len(terms) > 1:
        terms = [
            terms[i] + terms[i + 1] if i + 1 < len(terms) else terms[i] for i in range(0, len(terms), 2)
        ]
    return terms[0]


def spread(value):
    return jnp.broadcast_to(value, (SUB, BLOCK))


def small_inverse(entries):
    rest = [row[:] for row in entries]
    inverse = [None] * SUB
    upper = [[None] * SUB for _ in range(SUB)]
    for j in range(SUB):
        inverse[j] = lax.rsqrt(rest[j][j])
        for k in range(j + 1, SUB):
            upper[j][k] = rest[j][k] * inverse[j]
        for i in range(j + 1, SUB):
            for k in range(i, SUB):
                rest[i][k] = rest[i][k] - upper[j][i] * upper[j][k]
    result = [[None] * SUB for _ in range(SUB)]
    for j in range(SUB):
        result[j][j] = inverse[j]
        for i in range(j + 1, SUB):
            total = upper[j][i] * result[j][j]
            for k in range(j + 1, i):
                total = total + upper[k][i] * result[k][j]
            result[i][j] = -(inverse[i] * total)
    return result


def in_three(value):
    first = value.astype(bf16)
    rest = value - first.astype(f32)
    second = rest.astype(bf16)
    return first, second, (rest - second.astype(f32)).astype(bf16)


def exact(left, right, left_dim, right_dim):
    a, b, c = in_three(left)
    d, e, f = in_three(right)
    lefts = jnp.concatenate([a, a, b, b, a, c], axis=left_dim)
    rights = jnp.concatenate([d, e, d, e, f, d], axis=right_dim)
    return product(lefts, rights, left_dim, right_dim)


def factor_block(held):
    sub = lax.broadcasted_iota(jnp.int32, (SUB, BLOCK), 0)
    lane = lax.broadcasted_iota(jnp.int32, (SUB, BLOCK), 1)
    lane_row = lax.broadcasted_iota(jnp.int32, (1, BLOCK), 1)
    rows, following = held[:SUB, :], held[SUB : 2 * SUB, :]
    for lo in range(0, BLOCK, SUB):
        inside = (lane >= lo) & (lane < lo + SUB)
        lanes = [spread(rows[:, lo + k : lo + k + 1]) for k in range(SUB)]
        entries = [[spread(lanes[k][i : i + 1, :]) if k >= i else None for k in range(SUB)] for i in range(SUB)]
        inverse = small_inverse(entries)
        bare = [
            jnp.where(lane == lo + k, 1.0, jnp.where(inside, 0.0, spread(rows[k : k + 1, :]))) for k in range(SUB)
        ]
        done = [added([inverse[i][k] * bare[k] for k in range(i + 1)]) for i in range(SUB)]
        packed = done[0]
        for i in range(1, SUB):
            packed = jnp.where(sub == i, done[i], packed)
        held[lo : lo + SUB, :] = packed
        if lo + SUB < BLOCK:
            weights = [added([inverse[m][k] * done[m] for m in range(k, SUB)]) for k in range(SUB)]

            def brought(later):
                terms = [spread(later[:, lo + k : lo + k + 1]) * weights[k] for k in range(SUB)]
                return jnp.where(inside, 0.0, later) - added(terms)

            rows = brought(following)
        if lo + 2 * SUB < BLOCK:
            following = brought(held[lo + 2 * SUB : lo + 3 * SUB, :])
        if lo + 3 * SUB < BLOCK:
            change = exact(packed, packed, 0, 0)
            kept = jnp.where((lane_row >= lo) & (lane_row < lo + SUB), 0.0, held[lo + 3 * SUB :, :])
            held[lo + 3 * SUB :, :] = kept - change[lo + 3 * SUB :, :]


FIRST = {pair: n * BLOCK for n, pair in enumerate(PAIRS)}


def eliminate(b, own, gram, inverse):
    def block(i, j):
        return gram[FIRST[i, j] : FIRST[i, j] + BLOCK, :]

    lo, hi = b * BLOCK, (b + 1) * BLOCK
    if b:
        inverse[lo:hi, :lo] = exact(own, inverse[lo:hi, :lo], 1, 0)
    inverse[lo:hi, lo:hi] = own
    lower = {i: exact(block(i, b), own, 1, 1) for i in range(b + 1, BLOCKS)}
    for i in range(b + 1, BLOCKS):
        for j in range(b + 1, i + 1):
            gram[FIRST[i, j] : FIRST[i, j] + BLOCK, :] = block(i, j) - exact(lower[i], lower[j], 1, 1)
        into = slice(i * BLOCK, (i + 1) * BLOCK)
        inverse[into, :hi] = inverse[into, :hi] - exact(lower[i], inverse[lo:hi, :hi], 1, 0)


def inverse_kernel(place_ref, own_ref, other_ref, high_ref, low_ref, gram, inverse, held):
    for n in range(2 * FAR):
        source = own_ref if n < FAR else other_ref
        into = pl.multiple_of(place_ref[n] * SHARE, SUB)
        gram[pl.ds(into, SHARE), :] = source[(n % FAR) * SHARE : (n % FAR + 1) * SHARE, :]
    inverse[...] = jnp.zeros_like(inverse)
    row = lax.broadcasted_iota(jnp.int32, (BLOCK, BLOCK), 0)
    column = lax.broadcasted_iota(jnp.int32, (BLOCK, BLOCK), 1)

    @pl.loop(0, BLOCKS)
    def _(b):
        first = pl.multiple_of((b * (b + 1) // 2 + b) * BLOCK, BLOCK)
        held[...] = gram[pl.ds(first, BLOCK), :]
        factor_block(held)
        own = jnp.where(column <= row, held[...], 0.0)
        for step in range(BLOCKS):

            @pl.when(b == step)
            def _():
                eliminate(step, own, gram, inverse)

    high = inverse[...].astype(bf16)
    high_ref[...] = high
    low_ref[...] = (inverse[...] - high.astype(f32)).astype(bf16)


def kernel_call(kernel, place, inputs, outputs, scratch, flops):
    whole = pl.BlockSpec(memory_space=pltpu.VMEM)
    return pl.pallas_call(
        kernel,
        out_shape=outputs,
        in_specs=[pl.BlockSpec(memory_space=pltpu.SMEM)] + [whole] * len(inputs),
        out_specs=[whole] * len(outputs),
        scratch_shapes=[pltpu.VMEM(*one) for one in scratch],
        compiler_params=pltpu.CompilerParams(vmem_limit_bytes=12 << 20),
        cost_estimate=pl.CostEstimate(flops=flops, bytes_accessed=2 << 20, transcendentals=0),
    )(place, *inputs)


def inverse_factor(place, own, other):
    return kernel_call(
        inverse_kernel,
        place,
        (own, other),
        [jax.ShapeDtypeStruct((R, R), bf16)] * 2,
        [((len(PAIRS) * BLOCK, BLOCK), f32), ((R, R), f32), ((BLOCK, BLOCK), f32)],
        20 * R**3,
    )


def arrange(place, inputs, rows):
    def kernel(place_ref, *refs):
        n = 0
        for source in refs[:-1]:
            for lo in range(0, source.shape[0], rows):
                into = pl.multiple_of(place_ref[n] * rows, rows)
                refs[-1][pl.ds(into, rows), :] = source[lo : lo + rows, :]
                n += 1

    height = sum(value.shape[0] for value in inputs)
    output = jax.ShapeDtypeStruct((height, inputs[0].shape[1]), inputs[0].dtype)
    return kernel_call(kernel, place, inputs, [output], [], 1 << 20)[0]


def right_kernel(place_ref, high_ref, low_ref, *refs):
    pieces, (right_ref, own_ref, sums_ref, raw) = refs[:4], refs[4:]
    quarter = R // 4
    for n in range(4):
        into = pl.multiple_of(place_ref[n] * quarter, quarter)
        raw[pl.ds(into, quarter), :] = pieces[n][...]
    rows = own_ref.shape[0]
    mine = pl.ds(pl.multiple_of(place_ref[4] * rows, rows), rows)
    both = jnp.concatenate([high_ref[...], low_ref[...], high_ref[mine, :], low_ref[mine, :]])
    folded = []
    for lo in range(0, raw.shape[1], 2 * BLOCK):
        band = slice(lo, min(lo + 2 * BLOCK, raw.shape[1]))
        parts = product(both, raw[:, band], 1, 0)
        right = parts[:R, :] + parts[R : 2 * R, :]
        right_ref[:, band] = right.astype(bf16)
        own_ref[:, band] = parts[2 * R : 2 * R + rows, :] + parts[2 * R + rows :, :]
        square = right * right
        folded += [square[:, at : at + BLOCK] for at in range(0, right.shape[1], BLOCK)]
    row = jnp.sum(added(folded).T, axis=0, keepdims=True)
    sums_ref[...] = jnp.broadcast_to(row[None], sums_ref.shape)


def right_side(place, high, low, pieces, rows):
    width = pieces[0].shape[1]
    return kernel_call(
        right_kernel,
        place,
        (high, low, *pieces),
        [
            jax.ShapeDtypeStruct((R, width), bf16),
            jax.ShapeDtypeStruct((rows, width), f32),
            jax.ShapeDtypeStruct((2 * FAR, 1, R), f32),
        ],
        [((R, width), bf16)],
        4 * R * R * width,
    )


def update_kernel(place_ref, left_ref, right_ref, own_ref, sums_ref, update_ref, factor_ref, inverse):
    step = pl.program_id(0)

    @pl.when(step == 0)
    def _():
        norms = lax.rsqrt(jnp.sum(sums_ref[...], axis=0) + epsilon)
        inverse[...] = norms * math.sqrt(D * FF / R)
        rows = own_ref.shape[0]
        lane = lax.broadcasted_iota(jnp.int32, (rows, R), 1)
        row = lax.broadcasted_iota(jnp.int32, (rows, R), 0) + place_ref[4] * rows
        scale = jnp.sum(jnp.where(lane == row, norms, 0.0), axis=1, keepdims=True)
        factor_ref[...] = own_ref[...] * scale

    band = update_ref.shape[0]
    left = left_ref[pl.ds(pl.multiple_of(step * band, band), band), :]
    scaled = (left.astype(f32) * inverse[...]).astype(bf16)
    update_ref[...] = product(scaled, right_ref[...], 1, 0).astype(bf16)


def update_side(place, left, right, own, sums):
    height, width = left.shape[0], right.shape[1]
    steps = 2
    whole = pl.BlockSpec(memory_space=pltpu.VMEM)
    return pl.pallas_call(
        update_kernel,
        grid=(steps,),
        out_shape=[jax.ShapeDtypeStruct((height, width), bf16), jax.ShapeDtypeStruct(own.shape, f32)],
        in_specs=[pl.BlockSpec(memory_space=pltpu.SMEM)] + [whole] * 4,
        out_specs=[
            pl.BlockSpec((height // steps, width), lambda i: (i, 0)),
            pl.BlockSpec(own.shape, lambda i: (0, 0)),
        ],
        scratch_shapes=[pltpu.VMEM((1, R), f32)],
        compiler_params=pltpu.CompilerParams(vmem_limit_bytes=12 << 20),
        cost_estimate=pl.CostEstimate(flops=2 * R * height * width, bytes_accessed=4 << 20, transcendentals=0),
    )(place, left, right, own, sums)


def from_everyone(value, axis):
    length = lax.axis_size(axis)
    return lax.all_to_all(jnp.broadcast_to(value[None], (length, *value.shape)), axis, 0, 0, tiled=True)


def from_ahead(value, axis, steps):
    length = lax.axis_size(axis)
    return lax.ppermute(value, axis, [(i, (i - steps) % length) for i in range(length)])


def ahead(value, axis):
    return [value] + [from_ahead(value, axis, steps) for steps in range(1, lax.axis_size(axis))]


def exchanged(value, axis, index):
    count = lax.axis_size(axis)
    length = value.shape[0] // count
    pieces = [lax.dynamic_slice_in_dim(value, (index + k) % count * length, length, 0) for k in range(count)]
    return [pieces[0]] + [from_ahead(pieces[count - k], axis, k) for k in range(1, count)]


def total(pieces):
    return sum((value.astype(f32) for value in pieces[1:]), pieces[0].astype(f32))


def on_device(momentum, gradient, factor):
    z_hi, y, x, z_lo, core = (lax.axis_index(name) for name in ("z_hi", "y", "x", "z_lo", "core"))
    columns = factor.shape[1]
    gram_place = jnp.stack(
        [(core + c) % 2 * FAR + (x + j) % 4 * 4 + i for c in range(2) for j in range(4) for i in range(4)]
    ).astype(jnp.int32)
    left_place = jnp.stack([(core + c) % 2 * 4 + (x + j) % 4 for c in range(2) for j in range(4)]).astype(jnp.int32)
    fsdp_place = jnp.stack([(z_hi + h) % 2 * 4 + (y + k) % 4 for h in range(2) for k in range(4)]).astype(jnp.int32)
    row_group = z_hi * 4 + y
    right_place = jnp.stack([(y + k) % 4 for k in range(4)] + [row_group]).astype(jnp.int32)

    lowered = factor.T.astype(bf16)
    near = ahead(lowered, "y")
    across = ahead(from_ahead(lowered, "z_hi", 1), "y")
    all_lowered = arrange(fsdp_place, near + across, columns)
    blended = (momentum.astype(f32) + gradient.astype(f32)).astype(bf16)
    half = blended.shape[0] // 2
    own_rows = lax.dynamic_slice_in_dim(blended, core * half, half, 0)
    other_rows = lax.dynamic_slice_in_dim(blended, (1 - core) * half, half, 0)

    sent = product(other_rows, all_lowered, 1, 1).astype(bf16)
    arrived = from_ahead(sent, "core", 1)
    kept = lax.optimization_barrier(product(own_rows, all_lowered, 1, 1))
    partial_left = (kept + arrived.astype(f32)).astype(bf16)
    left_line = total(exchanged(partial_left, "x", x)).astype(bf16)
    left_rows = total(exchanged(left_line, "z_lo", z_lo)).astype(bf16)
    left_line = from_everyone(left_rows, "z_lo").reshape(half // 4, R)
    own_left = jnp.concatenate(ahead(left_line, "x"))
    other_left = from_ahead(own_left, "core", 1)

    local_gram = product(own_left, own_left, 0, 0) + product(other_left, other_left, 0, 0)
    packed = jnp.concatenate(
        [local_gram[i * BLOCK : (i + 1) * BLOCK, j * BLOCK : (j + 1) * BLOCK] for i, j in PAIRS]
    )
    piece = lax.dynamic_slice_in_dim(packed, (core * FAR + x * 4 + z_lo) * SHARE, SHARE, 0)
    summed = jnp.sum(from_everyone(piece, ("z_hi", "y")), axis=0)

    left_factor = arrange(left_place, (own_left, other_left), half // 4)
    partial_right = product(left_factor, blended, 0, 0).astype(bf16)
    received = exchanged(partial_right, "y", y)

    gram_line = from_everyone(summed, "z_lo").reshape(4 * SHARE, BLOCK)
    gram_line, *received = lax.optimization_barrier((gram_line, *received))
    right_rows = total(received).astype(bf16)
    gram_line, right_rows = lax.optimization_barrier((gram_line, right_rows))
    opposite = from_ahead(right_rows, "z_hi", 1)
    opposite, *gram_lines = lax.optimization_barrier((opposite, *ahead(gram_line, "x")))
    own_gram = jnp.concatenate(gram_lines)
    other_gram = from_ahead(own_gram, "core", 1)
    right_rows = total([right_rows, opposite]).astype(bf16)
    other_gram, right_rows = lax.optimization_barrier((other_gram, right_rows))
    right_pieces = ahead(right_rows, "y")
    high, low = inverse_factor(gram_place, own_gram, other_gram)
    right_factor, own_right, own_sums = right_side(right_place, high, low, right_pieces, columns)

    last_left = left_factor
    sums = lax.all_to_all(own_sums, TENSOR, 0, 0, tiled=True)
    orthonormal = (product(last_left, high, 1, 1) + product(last_left, low, 1, 1)).astype(bf16)
    taken = product(orthonormal, right_factor, 1, 0)
    new_momentum = (blended.astype(f32) - (1.0 - decay_rate) * taken).astype(bf16)
    update, own_factor = update_side(right_place, orthonormal, right_factor, own_right, sums)
    return (new_momentum, own_factor.T, update)


def solution(mesh):
    torus = Mesh(mesh.devices.reshape(2, 4, 4, 4, 2), ("z_hi", "y", "x", "z_lo", "core"))
    fsdp = ("z_hi", "y")
    return jax.shard_map(
        on_device,
        mesh=torus,
        in_specs=(P(fsdp, TENSOR), P(fsdp, TENSOR), P(TENSOR, fsdp)),
        out_specs=(P(fsdp, TENSOR), P(TENSOR, fsdp), P(fsdp, TENSOR)),
        check_vma=False,
    )
```

```python
import math

import jax
import jax.numpy as jnp
from jax import lax
from jax.experimental import pallas as pl
from jax.experimental.pallas import tpu as pltpu
from jax.sharding import Mesh
from jax.sharding import PartitionSpec as P

D = 8192
FF = 28672
R = 512
FAR = 16
BLOCK = 128
BLOCKS = R // BLOCK
PAIRS = [(i, j) for i in range(BLOCKS) for j in range(i + 1)]
SHARE = len(PAIRS) * BLOCK // (2 * FAR)
SUB = 8
TENSOR = ("x", "z_lo", "core")

decay_rate = 0.95
epsilon = 1e-06
f32 = jnp.float32
bf16 = jnp.bfloat16


def product(left, right, left_dim, right_dim):
    return lax.dot_general(left, right, (((left_dim,), (right_dim,)), ((), ())), preferred_element_type=f32)


def added(terms):
    while len(terms) > 1:
        terms = [
            terms[i] + terms[i + 1] if i + 1 < len(terms) else terms[i] for i in range(0, len(terms), 2)
        ]
    return terms[0]


def spread(value):
    return jnp.broadcast_to(value, (SUB, BLOCK))


def small_inverse(entries):
    rest = [row[:] for row in entries]
    inverse = [None] * SUB
    upper = [[None] * SUB for _ in range(SUB)]
    for j in range(SUB):
        inverse[j] = lax.rsqrt(rest[j][j])
        for k in range(j + 1, SUB):
            upper[j][k] = rest[j][k] * inverse[j]
        for i in range(j + 1, SUB):
            for k in range(i, SUB):
                rest[i][k] = rest[i][k] - upper[j][i] * upper[j][k]
    result = [[None] * SUB for _ in range(SUB)]
    for j in range(SUB):
        result[j][j] = inverse[j]
        for i in range(j + 1, SUB):
            total = upper[j][i] * result[j][j]
            for k in range(j + 1, i):
                total = total + upper[k][i] * result[k][j]
            result[i][j] = -(inverse[i] * total)
    return result


def in_three(value):
    first = value.astype(bf16)
    rest = value - first.astype(f32)
    second = rest.astype(bf16)
    return first, second, (rest - second.astype(f32)).astype(bf16)


def exact(left, right, left_dim, right_dim):
    a, b, c = in_three(left)
    d, e, f = in_three(right)
    lefts = jnp.concatenate([a, a, b, b, a, c], axis=left_dim)
    rights = jnp.concatenate([d, e, d, e, f, d], axis=right_dim)
    return product(lefts, rights, left_dim, right_dim)


def factor_block(held):
    sub = lax.broadcasted_iota(jnp.int32, (SUB, BLOCK), 0)
    lane = lax.broadcasted_iota(jnp.int32, (SUB, BLOCK), 1)
    lane_row = lax.broadcasted_iota(jnp.int32, (1, BLOCK), 1)
    rows, following = held[:SUB, :], held[SUB : 2 * SUB, :]
    for lo in range(0, BLOCK, SUB):
        inside = (lane >= lo) & (lane < lo + SUB)
        lanes = [spread(rows[:, lo + k : lo + k + 1]) for k in range(SUB)]
        entries = [[spread(lanes[k][i : i + 1, :]) if k >= i else None for k in range(SUB)] for i in range(SUB)]
        inverse = small_inverse(entries)
        bare = [
            jnp.where(lane == lo + k, 1.0, jnp.where(inside, 0.0, spread(rows[k : k + 1, :]))) for k in range(SUB)
        ]
        done = [added([inverse[i][k] * bare[k] for k in range(i + 1)]) for i in range(SUB)]
        packed = done[0]
        for i in range(1, SUB):
            packed = jnp.where(sub == i, done[i], packed)
        held[lo : lo + SUB, :] = packed
        if lo + SUB < BLOCK:
            weights = [added([inverse[m][k] * done[m] for m in range(k, SUB)]) for k in range(SUB)]

            def brought(later):
                terms = [spread(later[:, lo + k : lo + k + 1]) * weights[k] for k in range(SUB)]
                return jnp.where(inside, 0.0, later) - added(terms)

            rows = brought(following)
        if lo + 2 * SUB < BLOCK:
            following = brought(held[lo + 2 * SUB : lo + 3 * SUB, :])
        if lo + 3 * SUB < BLOCK:
            change = exact(packed, packed, 0, 0)
            kept = jnp.where((lane_row >= lo) & (lane_row < lo + SUB), 0.0, held[lo + 3 * SUB :, :])
            held[lo + 3 * SUB :, :] = kept - change[lo + 3 * SUB :, :]


FIRST = {pair: n * BLOCK for n, pair in enumerate(PAIRS)}


def eliminate(b, own, gram, inverse):
    def block(i, j):
        return gram[FIRST[i, j] : FIRST[i, j] + BLOCK, :]

    lo, hi = b * BLOCK, (b + 1) * BLOCK
    if b:
        inverse[lo:hi, :lo] = exact(own, inverse[lo:hi, :lo], 1, 0)
    inverse[lo:hi, lo:hi] = own
    lower = {i: exact(block(i, b), own, 1, 1) for i in range(b + 1, BLOCKS)}
    for i in range(b + 1, BLOCKS):
        for j in range(b + 1, i + 1):
            gram[FIRST[i, j] : FIRST[i, j] + BLOCK, :] = block(i, j) - exact(lower[i], lower[j], 1, 1)
        into = slice(i * BLOCK, (i + 1) * BLOCK)
        inverse[into, :hi] = inverse[into, :hi] - exact(lower[i], inverse[lo:hi, :hi], 1, 0)


def inverse_kernel(place_ref, own_ref, other_ref, high_ref, low_ref, gram, inverse, held):
    for n in range(2 * FAR):
        source = own_ref if n < FAR else other_ref
        into = pl.multiple_of(place_ref[n] * SHARE, SUB)
        gram[pl.ds(into, SHARE), :] = source[(n % FAR) * SHARE : (n % FAR + 1) * SHARE, :]
    inverse[...] = jnp.zeros_like(inverse)
    row = lax.broadcasted_iota(jnp.int32, (BLOCK, BLOCK), 0)
    column = lax.broadcasted_iota(jnp.int32, (BLOCK, BLOCK), 1)

    @pl.loop(0, BLOCKS)
    def _(b):
        first = pl.multiple_of((b * (b + 1) // 2 + b) * BLOCK, BLOCK)
        held[...] = gram[pl.ds(first, BLOCK), :]
        factor_block(held)
        own = jnp.where(column <= row, held[...], 0.0)
        for step in range(BLOCKS):

            @pl.when(b == step)
            def _():
                eliminate(step, own, gram, inverse)

    high = inverse[...].astype(bf16)
    high_ref[...] = high
    low_ref[...] = (inverse[...] - high.astype(f32)).astype(bf16)


def kernel_call(kernel, place, inputs, outputs, scratch, flops):
    whole = pl.BlockSpec(memory_space=pltpu.VMEM)
    return pl.pallas_call(
        kernel,
        out_shape=outputs,
        in_specs=[pl.BlockSpec(memory_space=pltpu.SMEM)] + [whole] * len(inputs),
        out_specs=[whole] * len(outputs),
        scratch_shapes=[pltpu.VMEM(*one) for one in scratch],
        compiler_params=pltpu.CompilerParams(vmem_limit_bytes=12 << 20),
        cost_estimate=pl.CostEstimate(flops=flops, bytes_accessed=2 << 20, transcendentals=0),
    )(place, *inputs)


def inverse_factor(place, own, other):
    return kernel_call(
        inverse_kernel,
        place,
        (own, other),
        [jax.ShapeDtypeStruct((R, R), bf16)] * 2,
        [((len(PAIRS) * BLOCK, BLOCK), f32), ((R, R), f32), ((BLOCK, BLOCK), f32)],
        20 * R**3,
    )


def arrange(place, inputs, rows):
    def kernel(place_ref, *refs):
        n = 0
        for source in refs[:-1]:
            for lo in range(0, source.shape[0], rows):
                into = pl.multiple_of(place_ref[n] * rows, rows)
                refs[-1][pl.ds(into, rows), :] = source[lo : lo + rows, :]
                n += 1

    height = sum(value.shape[0] for value in inputs)
    output = jax.ShapeDtypeStruct((height, inputs[0].shape[1]), inputs[0].dtype)
    return kernel_call(kernel, place, inputs, [output], [], 1 << 20)[0]


def right_kernel(place_ref, high_ref, low_ref, *refs):
    pieces, (right_ref, own_ref, sums_ref, raw) = refs[:4], refs[4:]
    quarter = R // 4
    for n in range(4):
        into = pl.multiple_of(place_ref[n] * quarter, quarter)
        raw[pl.ds(into, quarter), :] = pieces[n][...]
    rows = own_ref.shape[0]
    mine = pl.ds(pl.multiple_of(place_ref[4] * rows, rows), rows)
    both = jnp.concatenate([high_ref[...], low_ref[...], high_ref[mine, :], low_ref[mine, :]])
    folded = []
    for lo in range(0, raw.shape[1], 2 * BLOCK):
        band = slice(lo, min(lo + 2 * BLOCK, raw.shape[1]))
        parts = product(both, raw[:, band], 1, 0)
        right = parts[:R, :] + parts[R : 2 * R, :]
        right_ref[:, band] = right.astype(bf16)
        own_ref[:, band] = parts[2 * R : 2 * R + rows, :] + parts[2 * R + rows :, :]
        square = right * right
        folded += [square[:, at : at + BLOCK] for at in range(0, right.shape[1], BLOCK)]
    row = jnp.sum(added(folded).T, axis=0, keepdims=True)
    sums_ref[...] = jnp.broadcast_to(row[None], sums_ref.shape)


def right_side(place, high, low, pieces, rows):
    width = pieces[0].shape[1]
    return kernel_call(
        right_kernel,
        place,
        (high, low, *pieces),
        [
            jax.ShapeDtypeStruct((R, width), bf16),
            jax.ShapeDtypeStruct((rows, width), f32),
            jax.ShapeDtypeStruct((2 * FAR, 1, R), f32),
        ],
        [((R, width), bf16)],
        4 * R * R * width,
    )


def update_kernel(place_ref, left_ref, right_ref, own_ref, sums_ref, update_ref, factor_ref, inverse):
    step = pl.program_id(0)

    @pl.when(step == 0)
    def _():
        norms = lax.rsqrt(jnp.sum(sums_ref[...], axis=0) + epsilon)
        inverse[...] = norms * math.sqrt(D * FF / R)
        rows = own_ref.shape[0]
        lane = lax.broadcasted_iota(jnp.int32, (rows, R), 1)
        row = lax.broadcasted_iota(jnp.int32, (rows, R), 0) + place_ref[4] * rows
        scale = jnp.sum(jnp.where(lane == row, norms, 0.0), axis=1, keepdims=True)
        factor_ref[...] = own_ref[...] * scale

    band = update_ref.shape[0]
    left = left_ref[pl.ds(pl.multiple_of(step * band, band), band), :]
    scaled = (left.astype(f32) * inverse[...]).astype(bf16)
    update_ref[...] = product(scaled, right_ref[...], 1, 0).astype(bf16)


def update_side(place, left, right, own, sums):
    height, width = left.shape[0], right.shape[1]
    steps = 2
    whole = pl.BlockSpec(memory_space=pltpu.VMEM)
    return pl.pallas_call(
        update_kernel,
        grid=(steps,),
        out_shape=[jax.ShapeDtypeStruct((height, width), bf16), jax.ShapeDtypeStruct(own.shape, f32)],
        in_specs=[pl.BlockSpec(memory_space=pltpu.SMEM)] + [whole] * 4,
        out_specs=[
            pl.BlockSpec((height // steps, width), lambda i: (i, 0)),
            pl.BlockSpec(own.shape, lambda i: (0, 0)),
        ],
        scratch_shapes=[pltpu.VMEM((1, R), f32)],
        compiler_params=pltpu.CompilerParams(vmem_limit_bytes=12 << 20),
        cost_estimate=pl.CostEstimate(flops=2 * R * height * width, bytes_accessed=4 << 20, transcendentals=0),
    )(place, left, right, own, sums)


def from_everyone(value, axis):
    length = lax.axis_size(axis)
    return lax.all_to_all(jnp.broadcast_to(value[None], (length, *value.shape)), axis, 0, 0, tiled=True)


def from_ahead(value, axis, steps):
    length = lax.axis_size(axis)
    return lax.ppermute(value, axis, [(i, (i - steps) % length) for i in range(length)])


def ahead(value, axis):
    return [value] + [from_ahead(value, axis, steps) for steps in range(1, lax.axis_size(axis))]


def exchanged(value, axis, index):
    count = lax.axis_size(axis)
    length = value.shape[0] // count
    pieces = [lax.dynamic_slice_in_dim(value, (index + k) % count * length, length, 0) for k in range(count)]
    return [pieces[0]] + [from_ahead(pieces[count - k], axis, k) for k in range(1, count)]


def total(pieces):
    return sum((value.astype(f32) for value in pieces[1:]), pieces[0].astype(f32))


def on_device(momentum, gradient, factor):
    z_hi, y, x, z_lo, core = (lax.axis_index(name) for name in ("z_hi", "y", "x", "z_lo", "core"))
    columns = factor.shape[1]
    gram_place = jnp.stack(
        [(core + c) % 2 * FAR + (x + j) % 4 * 4 + (z_lo + i) % 4 for c in range(2) for j in range(4) for i in range(4)]
    ).astype(jnp.int32)
    core_place = jnp.stack([core, 1 - core]).astype(jnp.int32)
    fsdp_place = jnp.stack([(z_hi + h) % 2 * 4 + (y + k) % 4 for h in range(2) for k in range(4)]).astype(jnp.int32)
    row_group = z_hi * 4 + y
    right_place = jnp.stack([(y + k) % 4 for k in range(4)] + [row_group]).astype(jnp.int32)

    lowered = factor.T.astype(bf16)
    near = ahead(lowered, "y")
    across = ahead(from_ahead(lowered, "z_hi", 1), "y")
    all_lowered = arrange(fsdp_place, near + across, columns)
    blended = (momentum.astype(f32) + gradient.astype(f32)).astype(bf16)
    half = blended.shape[0] // 2
    own_rows = lax.dynamic_slice_in_dim(blended, core * half, half, 0)
    other_rows = lax.dynamic_slice_in_dim(blended, (1 - core) * half, half, 0)

    sent = product(other_rows, all_lowered, 1, 1).astype(bf16)
    arrived = from_ahead(sent, "core", 1)
    kept = lax.optimization_barrier(product(own_rows, all_lowered, 1, 1))
    partial_left = (kept + arrived.astype(f32)).astype(bf16)
    left_line = total(exchanged(partial_left, "x", x)).astype(bf16)
    left_rows = total(exchanged(left_line, "z_lo", z_lo)).astype(bf16)
    own_left = from_everyone(left_rows, ("x", "z_lo")).reshape(half, R)
    other_left = from_ahead(own_left, "core", 1)

    local_gram = product(own_left, own_left, 0, 0) + product(other_left, other_left, 0, 0)
    packed = jnp.concatenate(
        [local_gram[i * BLOCK : (i + 1) * BLOCK, j * BLOCK : (j + 1) * BLOCK] for i, j in PAIRS]
    )
    piece = lax.dynamic_slice_in_dim(packed, (core * FAR + x * 4 + z_lo) * SHARE, SHARE, 0)
    summed = jnp.sum(from_everyone(piece, ("z_hi", "y")), axis=0)

    left_factor = arrange(core_place, (own_left, other_left), half)
    partial_right = product(left_factor, blended, 0, 0).astype(bf16)
    received = exchanged(partial_right, "y", y)

    gram_line = jnp.concatenate(ahead(summed, "z_lo"))
    gram_line, *received = lax.optimization_barrier((gram_line, *received))
    right_rows = total(received).astype(bf16)
    gram_line, right_rows = lax.optimization_barrier((gram_line, right_rows))
    opposite = from_ahead(right_rows, "z_hi", 1)
    opposite, *gram_lines = lax.optimization_barrier((opposite, *ahead(gram_line, "x")))
    own_gram = jnp.concatenate(gram_lines)
    other_gram = from_ahead(own_gram, "core", 1)
    right_rows = total([right_rows, opposite]).astype(bf16)
    other_gram, right_rows = lax.optimization_barrier((other_gram, right_rows))
    right_pieces = ahead(right_rows, "y")
    high, low = inverse_factor(gram_place, own_gram, other_gram)
    right_factor, own_right, own_sums = right_side(right_place, high, low, right_pieces, columns)

    last_left = left_factor
    sums = lax.all_to_all(own_sums, TENSOR, 0, 0, tiled=True)
    orthonormal = (product(last_left, high, 1, 1) + product(last_left, low, 1, 1)).astype(bf16)
    taken = product(orthonormal, right_factor, 1, 0)
    new_momentum = (blended.astype(f32) - (1.0 - decay_rate) * taken).astype(bf16)
    update, own_factor = update_side(right_place, orthonormal, right_factor, own_right, sums)
    return (new_momentum, own_factor.T, update)


def solution(mesh):
    torus = Mesh(mesh.devices.reshape(2, 4, 4, 4, 2), ("z_hi", "y", "x", "z_lo", "core"))
    fsdp = ("z_hi", "y")
    return jax.shard_map(
        on_device,
        mesh=torus,
        in_specs=(P(fsdp, TENSOR), P(fsdp, TENSOR), P(TENSOR, fsdp)),
        out_specs=(P(fsdp, TENSOR), P(TENSOR, fsdp), P(fsdp, TENSOR)),
        check_vma=False,
    )
```
